32 devices in a mesh: band: 2 (over x), tm: 16 (over z, y, core).
Axes of the slice: x: 2, y: 2, z: 4, core: 2. Of those that a mesh axis runs over, the one named last changes fastest.
Arguments:
- voltages: bfloat16 [65536, 2048], P(('band', 'tm')), parts along dimension 0, may hold values from -6 to 6
- panel_map: int32 [2048], replicated, may hold values from 0 to 2047, each once
- block_list: int32 [16, 2], replicated, may hold values from 0 to 15, as said below
Outputs:
- visibilities: float32 [32, 2, 256, 128, 128], P('band', None, 'tm'), parts along dimension 0
The draws below stay inside these ranges and needn't reach their ends.
There are 2 independent parts, one for each index of `band`. The reference program is written for one: setup_inputs(seed, part) draws one part's arguments, and reference() takes and returns one part's arrays. A program takes and returns all parts, laid end to end along the dimension named above; an argument that names none is the same for every part. Nothing has to cross between parts.
Inputs may be any that keep to these rules, and one draw needn't show every extreme that they name: `block_list`: each row is a pair of panel numbers; the list names exactly 8 distinct panels, among them panel 0 and panel 16 - 1, every one of them in its first column.
All inputs are finite; a program needn't handle non-finite values.
Results may differ from the reference program's by a relative error of at most 0.0064.
Values may be sent and summed in bfloat16 or wider, within the bound.
No kernel may reach another device: no remote copies, remote signals or barrier semaphores. Data moves between devices by JAX's collectives and lax.ppermute only.
A program may use at most 128 MiB of HBM per device.

```python
import jax
import jax.numpy as jnp
from jax import lax

CHANNELS = 256
TAPS = 4
INP = 2048
PANEL = 128
USED = 8
NB = 16
PANELS = 16
SPECTRA = 64
SAMPLES = 32768


def draw_block_list(key, part):
    first_key = jax.random.fold_in(key, 11)
    second_key = jax.random.fold_in(key, 12)
    third_key = jax.random.fold_in(key, 13)
    middle = 1 + jax.random.permutation(first_key, PANELS - 2)[:USED - 2]
    ends_low = jnp.zeros((1,), jnp.int32)
    ends_high = jnp.full((1,), PANELS - 1, jnp.int32)
    picked = jnp.concatenate([ends_low, middle.astype(jnp.int32), ends_high], axis=0)
    chosen = jax.random.permutation(third_key, picked)
    picks = jax.random.randint(second_key, (NB,), 0, USED)
    cycle = jnp.arange(NB) % USED
    return jnp.stack([chosen[cycle], chosen[picks]], axis=1).astype(jnp.int32)


def level_of(own_key, shape, cuts, smallest, top_value):
    level = 1.0
    for axis_at, blocks in cuts:
        draws = jax.random.uniform(jax.random.fold_in(jax.random.fold_in(own_key, 6), axis_at), (blocks,), jnp.float32, smallest / len(cuts), top_value / len(cuts))
        level = level * jnp.repeat(jnp.exp(draws), shape[axis_at] // blocks).reshape((-1,) + (1,) * (len(shape) - 1 - axis_at))
    return level


def normal_values(key, dims, deviation, limit, split=(), kind=jnp.bfloat16):
    values = jax.random.normal(key, dims, jnp.float32) * deviation
    if len(split) > 0:
        values = level_of(key, dims, split, -0.22, 0.18) * values
    return jnp.clip(values, min=-limit, max=limit).astype(kind)


def setup_inputs(seed: int = 0, part: int = 0) -> dict:
    seeds = jax.random.split(jax.random.key(seed), 4)
    part_keys = jax.random.split(jax.random.fold_in(seeds[3], part), 4)
    voltages = normal_values(part_keys[0], (SAMPLES, INP), 1.0, 6.0, ((0, 16),))
    panel_map = jax.random.permutation(seeds[1], INP).astype(jnp.int32)
    block_list = draw_block_list(jax.random.fold_in(seeds[3], 71), part)
    return {"voltages": voltages, "panel_map": panel_map, "block_list": block_list}


def filter_taps(taps, frame):
    length = taps * frame
    place = jnp.arange(length).astype(jnp.float32)
    middle = (length - 1) / 2.0
    window = 0.5 - 0.5 * jnp.cos(2.0 * jnp.pi * (place + 0.5) / length)
    shape_h = jnp.sinc((place - middle) / frame) * window
    shape_h = shape_h / jnp.sqrt(jnp.sum(shape_h * shape_h))
    return shape_h.reshape(taps, frame).astype(jnp.float32)

def dft_table(channels):
    frame = 2 * channels
    rows_k = jnp.arange(channels, dtype=jnp.int32)[:, None]
    cols_n = jnp.arange(frame, dtype=jnp.int32)[None, :]
    phase = (rows_k * cols_n % frame).astype(jnp.float32) * (2.0 * jnp.pi / frame)
    return jnp.concatenate([jnp.cos(phase), -jnp.sin(phase)], axis=0).astype(jnp.bfloat16)

def reference(voltages, panel_map, block_list):
    frame = 2 * CHANNELS
    frames = voltages.reshape(SPECTRA, frame, INP)
    padded = jnp.concatenate([jnp.zeros((TAPS - 1, frame, INP), voltages.dtype), frames], axis=0)
    coeff = filter_taps(TAPS, frame)
    filtered = jnp.zeros((SPECTRA, frame, INP), jnp.float32)
    for tap in range(TAPS):
        filtered = filtered + coeff[tap][None, :, None] * padded[tap:tap + SPECTRA].astype(jnp.float32)
    filtered = filtered.astype(jnp.bfloat16)
    table = dft_table(CHANNELS)
    spectra = jnp.einsum('kn,sni->ski', table.astype(jnp.float32), filtered.astype(jnp.float32))
    spectra = spectra.astype(jnp.bfloat16).reshape(SPECTRA, 2, CHANNELS, INP)
    columns = panel_map.reshape(PANELS, PANEL)[block_list]

    def one_block(pair):
        first = spectra[:, :, :, pair[0]].astype(jnp.float32)
        second = spectra[:, :, :, pair[1]].astype(jnp.float32)
        flipped = jnp.stack([first[:, 1], -first[:, 0]], axis=1)
        real_part = jnp.einsum('scfi,scfj->fij', first, second)
        imag_part = jnp.einsum('scfi,scfj->fij', flipped, second)
        return jnp.stack([real_part, imag_part], axis=0) / SPECTRA
    return lax.map(one_block, columns)
```

```python
import functools

import jax
import jax.numpy as jnp
import numpy as np
from jax import lax
from jax.experimental import pallas as pl
from jax.experimental.pallas import tpu as pltpu
from jax.sharding import PartitionSpec as P

CHANNELS = 256
TAPS = 4
PANEL = 128
USED = 8
FRAME = 2 * CHANNELS
WIDTH = USED * PANEL
ROWS = 16
LANES = 256


def from_behind(block, axis, distance):
    devices = range(lax.axis_size(axis))
    route = [(i - distance, i) for i in devices if i - distance in devices]
    return lax.ppermute(block, axis, route)


def filter_taps():
    length = TAPS * FRAME
    place = np.arange(length, dtype=np.float64)
    middle = (length - 1) / 2.0
    window = 0.5 - 0.5 * np.cos(2.0 * np.pi * (place + 0.5) / length)
    shape_h = np.sinc((place - middle) / FRAME) * window
    shape_h = shape_h / np.sqrt(np.sum(shape_h * shape_h))
    taps = shape_h.reshape(TAPS, FRAME, 1).astype(np.float32)
    return np.broadcast_to(taps, (TAPS, FRAME, PANEL)).copy()


def dft_table(groups, parts):
    own = CHANNELS // groups
    per = own // parts
    q, g, f, c = np.meshgrid(
        np.arange(parts), np.arange(groups), np.arange(per), np.arange(2), indexing="ij"
    )
    channel = (g * own + q * per + f).reshape(-1)
    imaginary = c.reshape(-1)
    phase = (channel[:, None] * np.arange(FRAME)[None, :] % FRAME) * (2.0 * np.pi / FRAME)
    table = np.where(imaginary[:, None] == 1, -np.sin(phase), np.cos(phase))
    return table.astype(np.float32).astype(jnp.bfloat16)


def row_orders():
    pairs = 256 // ROWS
    half = ROWS // 2
    table = np.zeros((512, 256), np.float32)
    for j in range(pairs):
        for f in range(half):
            row, col = f * pairs * 2 + j * 2, j * ROWS + f * 2
            table[row, col] = 1.0
            table[row + 1, col + 1] = 1.0
            table[256 + row, col + 1] = -1.0
            table[256 + row + 1, col] = 1.0
    return table.astype(jnp.bfloat16)


def named_panels(blocks):
    bits = jnp.int32(0)
    for b in range(blocks.shape[0]):
        bits = bits | (jnp.int32(1) << blocks[b, 0])
    return bits


def filtered_frame(taps_ref, frames, cols):
    total = None
    taps = [jnp.tile(taps_ref[t], (1, cols // PANEL)) for t in range(TAPS)]
    for t in range(TAPS):
        term = taps[t] * frames[t].astype(jnp.float32)
        total = term if total is None else total + term
    return total.astype(jnp.bfloat16)


def select_kernel(blocks, volts, inputs, taps, table, chosen, first, hot, panels):
    step = pl.program_id(0)
    groups, parts = first.shape[0], first.shape[1]

    @pl.when(step == 0)
    def _():
        bits = named_panels(blocks)
        count = jnp.int32(0)
        for p in range(inputs.shape[0]):
            panels[count] = p
            count = count + ((bits >> p) & 1)
        for j in range(USED):
            wanted = inputs[pl.ds(panels[j], 1), :]
            rows = lax.broadcasted_iota(jnp.int32, (volts.shape[2], PANEL), 0)
            hot[:, j * PANEL : (j + 1) * PANEL] = (rows == wanted).astype(jnp.float32).astype(
                jnp.bfloat16
            )

    @pl.loop(0, WIDTH // LANES)
    def _(k):
        cols = pl.ds(pl.multiple_of(k * LANES, LANES), LANES)
        chosen[step, :, cols] = jnp.dot(
            volts[0], hot[:, cols], preferred_element_type=jnp.float32
        ).astype(jnp.bfloat16)

    @pl.when(step == TAPS - 1)
    def _():
        @pl.loop(0, WIDTH // LANES)
        def _(k):
            cols = pl.ds(pl.multiple_of(k * LANES, LANES), LANES)
            frames = [chosen[t, :, cols] for t in range(TAPS)]
            spectrum = jnp.dot(
                table[...],
                filtered_frame(taps, frames, LANES),
                preferred_element_type=jnp.float32,
            ).astype(jnp.bfloat16)
            for q in range(parts):
                for g in range(groups):
                    at = (q * groups + g) * ROWS
                    first[g, q, :, cols] = spectrum[at : at + ROWS]


def select(block_list, panel_map, frames, taps, table, groups, parts):
    count, frame, width = frames.shape
    return pl.pallas_call(
        select_kernel,
        grid_spec=pltpu.PrefetchScalarGridSpec(
            num_scalar_prefetch=1,
            grid=(count,),
            in_specs=[
                pl.BlockSpec((1, frame, width), lambda s, blocks: (s, 0, 0)),
                pl.BlockSpec((width // PANEL, PANEL), lambda s, blocks: (0, 0)),
                pl.BlockSpec((TAPS, frame, PANEL), lambda s, blocks: (0, 0, 0)),
                pl.BlockSpec((frame, frame), lambda s, blocks: (0, 0)),
            ],
            out_specs=[
                pl.BlockSpec((count, frame, WIDTH), lambda s, blocks: (0, 0, 0)),
                pl.BlockSpec((groups, parts, ROWS, WIDTH), lambda s, blocks: (0, 0, 0, 0)),
            ],
            scratch_shapes=[
                pltpu.VMEM((width, WIDTH), jnp.bfloat16),
                pltpu.SMEM((width // PANEL + 1,), jnp.int32),
            ],
        ),
        out_shape=[
            jax.ShapeDtypeStruct((count, frame, WIDTH), jnp.bfloat16),
            jax.ShapeDtypeStruct((groups, parts, ROWS, WIDTH), jnp.bfloat16),
        ],
        compiler_params=pltpu.CompilerParams(vmem_limit_bytes=48 << 20),
        cost_estimate=pl.CostEstimate(
            flops=2 * count * frame * width * WIDTH, bytes_accessed=14 << 20, transcendentals=0
        ),
        name="select",
    )(block_list, frames, panel_map.reshape(-1, PANEL), taps, table)


def spectra_kernel(earlier, own, taps, table, *out):
    groups = out[0].shape[0]
    depth = TAPS - 1
    cols = earlier.shape[2]
    pool = [earlier[t] for t in range(depth)] + [own[t] for t in range(depth)]
    for s in range(depth):
        spectrum = jnp.dot(
            table[...],
            filtered_frame(taps, pool[s : s + TAPS], cols),
            preferred_element_type=jnp.float32,
        ).astype(jnp.bfloat16)
        for q, part in enumerate(out):
            for g in range(groups):
                at = (q * groups + g) * ROWS
                part[g, s] = spectrum[at : at + ROWS]


def later_spectra(earlier, chosen, taps, table, groups, parts):
    depth = TAPS - 1
    frame = chosen.shape[1]
    return pl.pallas_call(
        spectra_kernel,
        grid=(WIDTH // LANES,),
        in_specs=[
            pl.BlockSpec((depth, frame, LANES), lambda k: (0, 0, k)),
            pl.BlockSpec((depth, frame, LANES), lambda k: (0, 0, k)),
            pl.BlockSpec((TAPS, frame, PANEL), lambda k: (0, 0, 0)),
            pl.BlockSpec((frame, frame), lambda k: (0, 0)),
        ],
        out_specs=[pl.BlockSpec((groups, depth, ROWS, LANES), lambda k: (0, 0, 0, k))] * parts,
        out_shape=[jax.ShapeDtypeStruct((groups, depth, ROWS, WIDTH), jnp.bfloat16)] * parts,
        compiler_params=pltpu.CompilerParams(vmem_limit_bytes=32 << 20),
        cost_estimate=pl.CostEstimate(
            flops=2 * depth * frame * frame * WIDTH, bytes_accessed=10 << 20, transcendentals=0
        ),
        name="later_spectra",
    )(earlier, chosen, taps, table)


def correlate_kernel(scale, blocks, first, rest, orders, *refs):
    out, plain, turned, across = refs[-4:]
    step = pl.program_id(0)
    per = ROWS // 2
    keys = 512 // per
    lead = first.shape[0] * ROWS // 256
    total = lead + rest.shape[0] // 256

    @pl.when(step == 0)
    def _():
        for n in range(total):
            rows = (
                first[pl.ds(n * 256 // ROWS, 256 // ROWS), 0].reshape(256, WIDTH)
                if n < lead
                else rest[pl.ds((n - lead) * 256, 256)]
            )
            moved = jnp.dot(orders[...], rows, preferred_element_type=jnp.float32).astype(
                jnp.bfloat16
            )
            width = 256 // per
            for f in range(per):
                plain[f, n * width : (n + 1) * width] = moved[f * width : (f + 1) * width]
                turned[f, n * width : (n + 1) * width] = moved[
                    256 + f * width : 256 + (f + 1) * width
                ]

    across[...] = plain[step].T
    bits = named_panels(blocks)

    def place(panel):
        below = bits & ((jnp.int32(1) << panel) - 1)
        count = jnp.int32(0)
        for p in range(16):
            count = count + ((below >> p) & 1)
        return pl.multiple_of(count * PANEL, PANEL)

    for b in range(blocks.shape[0]):
        a, w = place(blocks[b, 0]), place(blocks[b, 1])
        left = across[pl.ds(a, PANEL), :]
        right = jnp.concatenate(
            [plain[step, :, pl.ds(w, PANEL)], turned[step, :, pl.ds(w, PANEL)]], axis=1
        )
        product = jnp.dot(left, right, preferred_element_type=jnp.float32) * scale
        out[b, 0, 0] = product[:, :PANEL]
        out[b, 1, 0] = product[:, PANEL:]


def correlate(block_list, first, rest, orders, part, shape, so_far):
    groups, parts = first.shape[0], first.shape[1]
    per = ROWS // 2
    keys = 2 * groups * TAPS
    rest = rest.reshape(-1, WIDTH)
    blocks = shape[0]
    operands = [block_list, first, rest, orders]
    in_specs = [
        pl.BlockSpec((groups, 1, ROWS, WIDTH), lambda s, blocks: (0, part, 0, 0)),
        pl.BlockSpec(rest.shape, lambda s, blocks: (0, 0)),
        pl.BlockSpec(orders.shape, lambda s, blocks: (0, 0)),
    ]
    aliases = {}
    if so_far is not None:
        aliases = {len(operands): 0}
        operands.append(so_far)
        in_specs.append(pl.BlockSpec(memory_space=pl.ANY))
    return pl.pallas_call(
        functools.partial(correlate_kernel, 1.0 / (groups * TAPS)),
        grid_spec=pltpu.PrefetchScalarGridSpec(
            num_scalar_prefetch=1,
            grid=(per,),
            in_specs=in_specs,
            out_specs=pl.BlockSpec(
                (blocks, 2, 1, PANEL, PANEL), lambda s, blocks: (0, 0, part * per + s, 0, 0)
            ),
            scratch_shapes=[
                pltpu.VMEM((per, keys, WIDTH), jnp.bfloat16),
                pltpu.VMEM((per, keys, WIDTH), jnp.bfloat16),
                pltpu.VMEM((WIDTH, keys), jnp.bfloat16),
            ],
        ),
        out_shape=jax.ShapeDtypeStruct(shape, jnp.float32),
        input_output_aliases=aliases,
        compiler_params=pltpu.CompilerParams(vmem_limit_bytes=48 << 20),
        cost_estimate=pl.CostEstimate(
            flops=4 * per * keys * PANEL * PANEL * blocks,
            bytes_accessed=18 << 20,
            transcendentals=0,
        ),
        name="correlate",
    )(*operands)


def body(voltages, panel_map, block_list):
    groups = lax.axis_size("tm")
    own = CHANNELS // groups
    parts = own * 2 // ROWS
    frames = voltages.reshape(-1, FRAME, voltages.shape[1])
    taps = filter_taps()
    table = dft_table(groups, parts)
    chosen, first = select(block_list, panel_map, frames, taps, table, groups, parts)
    earlier = from_behind(chosen[1:], "tm", 1)
    exchange = functools.partial(
        lax.all_to_all, axis_name="tm", split_axis=0, concat_axis=0, tiled=True
    )
    first = exchange(first)
    rest = later_spectra(earlier, chosen, taps, table, groups, parts)
    rest = [exchange(part) for part in rest]
    shape = (block_list.shape[0], 2, own, PANEL, PANEL)
    out = None
    for q in range(parts):
        out = correlate(block_list, first, rest[q], row_orders(), q, shape, out)
    return out


def solution(mesh):
    in_specs = (P(("band", "tm"), None), P(), P())
    out_specs = P("band", None, "tm", None, None)
    return jax.shard_map(body, mesh=mesh, in_specs=in_specs, out_specs=out_specs, check_vma=False)
```

```python
import functools

import jax
import jax.numpy as jnp
import numpy as np
from jax import lax
from jax.experimental import pallas as pl
from jax.experimental.pallas import tpu as pltpu
from jax.sharding import PartitionSpec as P

CHANNELS = 256
TAPS = 4
PANEL = 128
USED = 8
FRAME = 2 * CHANNELS
WIDTH = USED * PANEL
ROWS = 16
LANES = 256
VMEM = 60 << 20


def pin(*arrays):
    return [pltpu.with_memory_space_constraint(array, pltpu.HBM) for array in arrays]


def shifted(block, axis, distance, around):
    count = lax.axis_size(axis)
    route = [(i, (i + distance) % count) for i in range(count) if around or 0 <= i + distance < count]
    return lax.ppermute(block, axis, route)


def filter_taps():
    length = TAPS * FRAME
    place = np.arange(length, dtype=np.float64)
    middle = (length - 1) / 2.0
    window = 0.5 - 0.5 * np.cos(2.0 * np.pi * (place + 0.5) / length)
    shape_h = np.sinc((place - middle) / FRAME) * window
    shape_h = shape_h / np.sqrt(np.sum(shape_h * shape_h))
    taps = shape_h.reshape(TAPS, FRAME, 1).astype(np.float32)
    return np.broadcast_to(taps, (TAPS, FRAME, PANEL)).copy()


def dft_table(groups, parts):
    own = CHANNELS // groups
    per = own // parts
    q, g, f, c = np.meshgrid(
        np.arange(parts), np.arange(groups), np.arange(per), np.arange(2), indexing="ij"
    )
    channel = (g * own + q * per + f).reshape(-1)
    imaginary = c.reshape(-1)
    phase = (channel[:, None] * np.arange(FRAME)[None, :] % FRAME) * (2.0 * np.pi / FRAME)
    table = np.where(imaginary[:, None] == 1, -np.sin(phase), np.cos(phase))
    return table.astype(np.float32).astype(jnp.bfloat16)


def row_orders():
    pairs = 256 // ROWS
    half = ROWS // 2
    table = np.zeros((512, 256), np.float32)
    for j in range(pairs):
        for f in range(half):
            row, col = f * pairs * 2 + j * 2, j * ROWS + f * 2
            table[row, col] = 1.0
            table[row + 1, col + 1] = 1.0
            table[256 + row, col + 1] = -1.0
            table[256 + row + 1, col] = 1.0
    return table.astype(jnp.bfloat16)


def named_panels(blocks):
    bits = jnp.int32(0)
    for b in range(blocks.shape[1]):
        bits = bits | (jnp.int32(1) << blocks[0, b])
    return bits


def filtered_frame(taps_ref, frames, cols):
    total = None
    taps = [jnp.tile(taps_ref[t], (1, cols // PANEL)) for t in range(TAPS)]
    for t in range(TAPS):
        term = taps[t] * frames[t].astype(jnp.float32)
        total = term if total is None else total + term
    return total.astype(jnp.bfloat16)


def select_kernel(
    blocks, frames, inputs, up, down, hot_out, places, volts, names, hot, chosen, panels, come, go
):
    depth = TAPS - 1
    half = WIDTH // 2
    listed = pltpu.make_async_copy(inputs, names, come.at[TAPS])
    listed.start()
    order = list(range(1, TAPS)) + [0]
    arrive = {t: pltpu.make_async_copy(frames.at[t], volts.at[t], come.at[t]) for t in order}
    for t in order:
        arrive[t].start()
    bits = named_panels(blocks)
    count = jnp.int32(0)
    slots = TAPS * USED
    for p in range(inputs.shape[0]):
        panels[count] = p
        panels[slots + p] = count * PANEL
        count = count + ((bits >> p) & 1)
    listed.wait()
    sends = []

    def send(source, target):
        sends.append(pltpu.make_async_copy(source, target, go.at[len(sends)]))
        sends[-1].start()

    for side in range(2):
        for j in range(side * USED // 2, (side + 1) * USED // 2):
            wanted = names[pl.ds(panels[j], 1), :]
            rows = lax.broadcasted_iota(jnp.int32, (volts.shape[2], PANEL), 0)
            hot[:, j * PANEL : (j + 1) * PANEL] = (
                (rows == wanted).astype(jnp.float32).astype(jnp.bfloat16)
            )
        cols = slice(side * half, (side + 1) * half)
        send(hot.at[:, cols], hot_out.at[:, cols])
        for t in range(depth):
            source = t if side else t + 1
            if source in arrive:
                arrive.pop(source).wait()
            chosen[t, :, cols] = jnp.dot(
                volts[source], hot[:, cols], preferred_element_type=jnp.float32
            ).astype(jnp.bfloat16)
            send(chosen.at[t, :, cols], (down if side else up).at[t])
    for i in range(2):
        for b in range(blocks.shape[1]):
            places[i, b] = panels[slots + blocks[i, b]]
    for copy in sends:
        copy.wait()


def select(block_list, panel_map, frames):
    count, frame, width = frames.shape
    depth = TAPS - 1
    anywhere = pl.BlockSpec(memory_space=pl.ANY)
    return pl.pallas_call(
        select_kernel,
        grid_spec=pltpu.PrefetchScalarGridSpec(
            num_scalar_prefetch=1,
            grid=(1,),
            in_specs=[anywhere] * 2,
            out_specs=[anywhere] * 3 + [pl.BlockSpec(memory_space=pltpu.SMEM)],
            scratch_shapes=[
                pltpu.VMEM((count, frame, width), jnp.bfloat16),
                pltpu.VMEM((width // PANEL, PANEL), jnp.int32),
                pltpu.VMEM((width, WIDTH), jnp.bfloat16),
                pltpu.VMEM((depth, frame, WIDTH), jnp.bfloat16),
                pltpu.SMEM((TAPS * USED + width // PANEL,), jnp.int32),
                pltpu.SemaphoreType.DMA((1 + TAPS,)),
                pltpu.SemaphoreType.DMA((2 + 2 * depth,)),
            ],
        ),
        out_shape=[
            pltpu.HBM((depth, frame, WIDTH // 2), jnp.bfloat16),
            pltpu.HBM((depth, frame, WIDTH // 2), jnp.bfloat16),
            pltpu.HBM((width, WIDTH), jnp.bfloat16),
            jax.ShapeDtypeStruct(block_list.shape, jnp.int32),
        ],
        compiler_params=pltpu.CompilerParams(vmem_limit_bytes=VMEM),
        cost_estimate=pl.CostEstimate(
            flops=3 * frame * width * WIDTH * 2, bytes_accessed=15 << 20, transcendentals=0
        ),
        name="select",
    )(block_list, *pin(frames, panel_map.reshape(-1, PANEL)))


def first_kernel(frame, hot, up, down, taps, table, extra, first):
    groups, parts = first.shape[0], first.shape[1]
    depth = TAPS - 1
    chosen = jnp.dot(frame[0], hot[...], preferred_element_type=jnp.float32).astype(jnp.bfloat16)
    extra[...] = chosen

    def spectra(frames):
        spectrum = jnp.dot(
            table[...],
            filtered_frame(taps, frames, chosen.shape[1]),
            preferred_element_type=jnp.float32,
        ).astype(jnp.bfloat16)
        for q in range(parts):
            for g in range(groups):
                at = (q * groups + g) * ROWS
                first[g, q] = spectrum[at : at + ROWS]

    left = pl.program_id(0) < pl.num_programs(0) // 2

    @pl.when(left)
    def _():
        spectra([extra[...]] + [up[t] for t in range(depth)])

    @pl.when(jnp.logical_not(left))
    def _():
        spectra([down[t] for t in range(depth)] + [extra[...]])


def first_spectra(frames, hot, up, down, taps, table, groups, parts):
    count, frame, width = frames.shape
    depth = TAPS - 1
    tiles = WIDTH // LANES // 2
    return pl.pallas_call(
        first_kernel,
        grid=(2 * tiles,),
        in_specs=[
            pl.BlockSpec((1, frame, width), lambda k: (k // tiles * (TAPS - 1), 0, 0)),
            pl.BlockSpec((width, LANES), lambda k: (0, k)),
            pl.BlockSpec((depth, frame, LANES), lambda k: (0, 0, jnp.minimum(k, tiles - 1))),
            pl.BlockSpec((depth, frame, LANES), lambda k: (0, 0, jnp.maximum(k - tiles, 0))),
            pl.BlockSpec((TAPS, frame, PANEL), lambda k: (0, 0, 0)),
            pl.BlockSpec((frame, frame), lambda k: (0, 0)),
        ],
        out_specs=[
            pl.BlockSpec((frame, LANES), lambda k: (0, k)),
            pl.BlockSpec((groups, parts, ROWS, LANES), lambda k: (0, 0, 0, k)),
        ],
        out_shape=[
            pltpu.HBM((frame, WIDTH), jnp.bfloat16),
            pltpu.HBM((groups, parts, ROWS, WIDTH), jnp.bfloat16),
        ],
        compiler_params=pltpu.CompilerParams(vmem_limit_bytes=VMEM // 2),
        cost_estimate=pl.CostEstimate(
            flops=2 * frame * (width + frame) * WIDTH, bytes_accessed=14 << 20, transcendentals=0
        ),
        name="first_spectra",
    )(*pin(frames, hot, up, down, taps, table))


def spectra_kernel(earlier, later, up, down, extra, taps, table, *out):
    groups = out[0].shape[0]
    depth = TAPS - 1
    cols = extra.shape[1]

    def spectra(pool):
        for s in range(depth):
            spectrum = jnp.dot(
                table[...],
                filtered_frame(taps, pool[s : s + TAPS], cols),
                preferred_element_type=jnp.float32,
            ).astype(jnp.bfloat16)
            for q, part in enumerate(out):
                for g in range(groups):
                    at = (q * groups + g) * ROWS
                    part[g, s] = spectrum[at : at + ROWS]

    left = pl.program_id(0) < pl.num_programs(0) // 2

    @pl.when(left)
    def _():
        own = [extra[...]] + [up[t] for t in range(depth - 1)]
        spectra([earlier[t] for t in range(depth)] + own)

    @pl.when(jnp.logical_not(left))
    def _():
        last = lax.axis_index("tm") == lax.axis_size("tm") - 1
        own = [down[t] for t in range(1, depth)] + [extra[...]]
        own = [jnp.where(last, jnp.zeros_like(frame), frame) for frame in own]
        spectra(own + [later[t] for t in range(depth)])


def later_spectra(earlier, later, up, down, extra, taps, table, groups, parts):
    depth = TAPS - 1
    frame = extra.shape[0]
    tiles = WIDTH // LANES // 2
    before = pl.BlockSpec((depth, frame, LANES), lambda k: (0, 0, jnp.minimum(k, tiles - 1)))
    after = pl.BlockSpec((depth, frame, LANES), lambda k: (0, 0, jnp.maximum(k - tiles, 0)))
    return pl.pallas_call(
        spectra_kernel,
        grid=(2 * tiles,),
        in_specs=[
            before,
            after,
            before,
            after,
            pl.BlockSpec((frame, LANES), lambda k: (0, k)),
            pl.BlockSpec((TAPS, frame, PANEL), lambda k: (0, 0, 0)),
            pl.BlockSpec((frame, frame), lambda k: (0, 0)),
        ],
        out_specs=[pl.BlockSpec((groups, depth, ROWS, LANES), lambda k: (0, 0, 0, k))] * parts,
        out_shape=[pltpu.HBM((groups, depth, ROWS, WIDTH), jnp.bfloat16)] * parts,
        compiler_params=pltpu.CompilerParams(vmem_limit_bytes=VMEM // 2),
        cost_estimate=pl.CostEstimate(
            flops=200 * depth * frame * frame * WIDTH, bytes_accessed=10 << 20, transcendentals=0
        ),
        name="later_spectra",
    )(earlier, later, *pin(up, down, extra, taps, table))


def same_frames(rest, n):
    behind = (TAPS - 1) * ROWS
    half, at = WIDTH // 2, n * 256
    left = rest[at : at + 256, :half]
    if n == 0:
        right = jnp.concatenate(
            [rest[rest.shape[0] - behind :, half:], rest[: 256 - behind, half:]], axis=0
        )
    else:
        right = rest[at - behind : at + 256 - behind, half:]
    return jnp.concatenate([left, right], axis=1)


def correlate_kernel(scale, blocks, first, rest, orders, *refs):
    out, plain, turned, across = refs[-4:]
    step = pl.program_id(0)
    per = ROWS // 2
    keys = 512 // per
    lead = first.shape[0] * ROWS // 256
    total = lead + rest.shape[0] // 256

    @pl.when(step == 0)
    def _():
        for n in range(total):
            rows = (
                first[pl.ds(n * 256 // ROWS, 256 // ROWS), 0].reshape(256, WIDTH)
                if n < lead
                else same_frames(rest, n - lead)
            )
            moved = jnp.dot(orders[...], rows, preferred_element_type=jnp.float32).astype(
                jnp.bfloat16
            )
            width = 256 // per
            for f in range(per):
                plain[f, n * width : (n + 1) * width] = moved[f * width : (f + 1) * width]
                turned[f, n * width : (n + 1) * width] = moved[
                    256 + f * width : 256 + (f + 1) * width
                ]

    across[...] = plain[step].T
    for b in range(blocks.shape[1]):
        a, w = (pl.multiple_of(blocks[i, b], PANEL) for i in range(2))
        left = across[pl.ds(a, PANEL), :]
        right = jnp.concatenate(
            [plain[step, :, pl.ds(w, PANEL)], turned[step, :, pl.ds(w, PANEL)]], axis=1
        )
        product = jnp.dot(left, right, preferred_element_type=jnp.float32) * scale
        out[b, 0, 0] = product[:, :PANEL]
        out[b, 1, 0] = product[:, PANEL:]


def correlate(places, first, rest, orders, part, shape, so_far):
    groups, parts = first.shape[0], first.shape[1]
    per = ROWS // 2
    keys = 2 * groups * TAPS
    rest = rest.reshape(-1, WIDTH)
    blocks = shape[0]
    operands = [places, first, rest, orders]
    in_specs = [
        pl.BlockSpec((groups, 1, ROWS, WIDTH), lambda s, blocks: (0, part, 0, 0)),
        pl.BlockSpec(rest.shape, lambda s, blocks: (0, 0)),
        pl.BlockSpec(orders.shape, lambda s, blocks: (0, 0)),
    ]
    aliases = {}
    if so_far is not None:
        aliases = {len(operands): 0}
        operands.append(so_far)
        in_specs.append(pl.BlockSpec(memory_space=pl.ANY))
    return pl.pallas_call(
        functools.partial(correlate_kernel, 1.0 / (groups * TAPS)),
        grid_spec=pltpu.PrefetchScalarGridSpec(
            num_scalar_prefetch=1,
            grid=(per,),
            in_specs=in_specs,
            out_specs=pl.BlockSpec(
                (blocks, 2, 1, PANEL, PANEL), lambda s, blocks: (0, 0, part * per + s, 0, 0)
            ),
            scratch_shapes=[
                pltpu.VMEM((per, keys, WIDTH), jnp.bfloat16),
                pltpu.VMEM((per, keys, WIDTH), jnp.bfloat16),
                pltpu.VMEM((WIDTH, keys), jnp.bfloat16),
            ],
        ),
        out_shape=jax.ShapeDtypeStruct(shape, jnp.float32),
        input_output_aliases=aliases,
        compiler_params=pltpu.CompilerParams(vmem_limit_bytes=VMEM // 2),
        cost_estimate=pl.CostEstimate(
            flops=4 * per * keys * PANEL * PANEL * blocks,
            bytes_accessed=18 << 20,
            transcendentals=0,
        ),
        name="correlate",
    )(*operands)


def body(voltages, panel_map, block_list):
    groups = lax.axis_size("tm")
    own = CHANNELS // groups
    parts = own * 2 // ROWS
    frames = voltages.reshape(-1, FRAME, voltages.shape[1])
    taps = filter_taps()
    table = dft_table(groups, parts)
    block_list = block_list.T
    up, down, hot, places = select(block_list, panel_map, frames)
    earlier = shifted(up, "tm", 1, False)
    later = shifted(down, "tm", -1, True)
    extra, first = first_spectra(frames, hot, up, down, taps, table, groups, parts)
    exchange = functools.partial(
        lax.all_to_all, axis_name="tm", split_axis=0, concat_axis=0, tiled=True
    )
    first = exchange(first)
    rest = later_spectra(earlier, later, up, down, extra, taps, table, groups, parts)
    rest = [exchange(part) for part in rest]
    shape = (block_list.shape[1], 2, own, PANEL, PANEL)
    out = None
    for q in range(parts):
        out = correlate(places, first, rest[q], row_orders(), q, shape, out)
    return out


def solution(mesh):
    in_specs = (P(("band", "tm"), None), P(), P())
    out_specs = P("band", None, "tm", None, None)
    return jax.shard_map(body, mesh=mesh, in_specs=in_specs, out_specs=out_specs, check_vma=False)
```

```python
import functools

import jax
import jax.numpy as jnp
import numpy as np
from jax import lax
from jax.experimental import pallas as pl
from jax.experimental.pallas import tpu as pltpu
from jax.sharding import PartitionSpec as P

CHANNELS = 256
TAPS = 4
PANEL = 128
USED = 8
FRAME = 2 * CHANNELS
WIDTH = USED * PANEL
ROWS = 16
LANES = 256
VMEM = 60 << 20


def pin(*arrays):
    return [pltpu.with_memory_space_constraint(array, pltpu.HBM) for array in arrays]


def shifted(block, axis, distance, around):
    count = lax.axis_size(axis)
    route = [(i, (i + distance) % count) for i in range(count) if around or 0 <= i + distance < count]
    return lax.ppermute(block, axis, route)


def filter_taps():
    length = TAPS * FRAME
    place = np.arange(length, dtype=np.float64)
    middle = (length - 1) / 2.0
    window = 0.5 - 0.5 * np.cos(2.0 * np.pi * (place + 0.5) / length)
    shape_h = np.sinc((place - middle) / FRAME) * window
    shape_h = shape_h / np.sqrt(np.sum(shape_h * shape_h))
    taps = shape_h.reshape(TAPS, FRAME, 1).astype(np.float32)
    return np.broadcast_to(taps, (TAPS, FRAME, PANEL)).copy()


def dft_table(groups, parts):
    own = CHANNELS // groups
    per = own // parts
    q, g, f, c = np.meshgrid(
        np.arange(parts), np.arange(groups), np.arange(per), np.arange(2), indexing="ij"
    )
    channel = (g * own + q * per + f).reshape(-1)
    imaginary = c.reshape(-1)
    phase = (channel[:, None] * np.arange(FRAME)[None, :] % FRAME) * (2.0 * np.pi / FRAME)
    table = np.where(imaginary[:, None] == 1, -np.sin(phase), np.cos(phase))
    return table.astype(np.float32).astype(jnp.bfloat16)


def row_orders():
    pairs = 256 // ROWS
    half = ROWS // 2
    table = np.zeros((512, 256), np.float32)
    for j in range(pairs):
        for f in range(half):
            row, col = f * pairs * 2 + j * 2, j * ROWS + f * 2
            table[row, col] = 1.0
            table[row + 1, col + 1] = 1.0
            table[256 + row, col + 1] = -1.0
            table[256 + row + 1, col] = 1.0
    return table.astype(jnp.bfloat16)


def named_panels(blocks):
    bits = jnp.int32(0)
    for b in range(blocks.shape[1]):
        bits = bits | (jnp.int32(1) << blocks[0, b])
    return bits


def filtered_frame(taps_ref, frames, cols):
    total = None
    taps = [jnp.tile(taps_ref[t], (1, cols // PANEL)) for t in range(TAPS)]
    for t in range(TAPS):
        term = taps[t] * frames[t].astype(jnp.float32)
        total = term if total is None else total + term
    return total.astype(jnp.bfloat16)


def select_kernel(side, blocks, frames, inputs, taps, table, *refs):
    halo, extra, first, places = refs[-14:-10]
    volts, names, weights, matrix, hot, chosen, spectra, panels, come, go = refs[-10:]
    groups, parts = first.shape[0], first.shape[1]
    half = WIDTH // 2
    order = [(t + 1 - side) % TAPS for t in range(TAPS)]
    listed = pltpu.make_async_copy(inputs, names, come.at[TAPS])
    listed.start()
    arrive = [pltpu.make_async_copy(frames.at[t], volts.at[t], come.at[t]) for t in order]
    arrive.append(pltpu.make_async_copy(taps, weights, come.at[TAPS + 1]))
    arrive.append(pltpu.make_async_copy(table, matrix, come.at[TAPS + 2]))
    for copy in arrive:
        copy.start()
    bits = named_panels(blocks)
    count = jnp.int32(0)
    slots = TAPS * USED
    for p in range(inputs.shape[0]):
        panels[count] = p
        panels[slots + p] = count * PANEL
        count = count + ((bits >> p) & 1)
    listed.wait()
    for j in range(USED // 2):
        wanted = names[pl.ds(panels[side * USED // 2 + j], 1), :]
        rows = lax.broadcasted_iota(jnp.int32, (volts.shape[2], PANEL), 0)
        hot[:, j * PANEL : (j + 1) * PANEL] = (
            (rows == wanted).astype(jnp.float32).astype(jnp.bfloat16)
        )
    sends = []

    def send(source, target):
        sends.append(pltpu.make_async_copy(source, target, go.at[len(sends)]))
        sends[-1].start()

    for k, t in enumerate(order):
        arrive[k].wait()
        chosen[t] = jnp.dot(volts[t], hot[...], preferred_element_type=jnp.float32).astype(
            jnp.bfloat16
        )
        send(chosen.at[t], halo.at[k] if k < TAPS - 1 else extra)
    arrive[TAPS].wait()
    arrive[TAPS + 1].wait()
    for k in range(half // LANES):
        cols = slice(k * LANES, (k + 1) * LANES)
        spectrum = jnp.dot(
            matrix[...],
            filtered_frame(weights, [chosen[t, :, cols] for t in range(TAPS)], LANES),
            preferred_element_type=jnp.float32,
        ).astype(jnp.bfloat16)
        for q in range(parts):
            for g in range(groups):
                at = (q * groups + g) * ROWS
                spectra[g, q, :, cols] = spectrum[at : at + ROWS]
    send(spectra, first.at[:, :, :, side * half : (side + 1) * half])
    for i in range(2):
        for b in range(blocks.shape[1]):
            places[i, b] = panels[slots + blocks[i, b]]
    for copy in sends:
        copy.wait()


def select(side, block_list, panel_map, frames, taps, table, groups, parts, so_far):
    count, frame, width = frames.shape
    depth = TAPS - 1
    half = WIDTH // 2
    anywhere = pl.BlockSpec(memory_space=pl.ANY)
    operands = [block_list, *pin(frames, panel_map.reshape(-1, PANEL), taps, table)]
    aliases = {}
    if so_far is not None:
        aliases = {len(operands): 2}
        operands.append(so_far)
    return pl.pallas_call(
        functools.partial(select_kernel, side),
        grid_spec=pltpu.PrefetchScalarGridSpec(
            num_scalar_prefetch=1,
            grid=(1,),
            in_specs=[anywhere] * (len(operands) - 1),
            out_specs=[anywhere] * 3 + [pl.BlockSpec(memory_space=pltpu.SMEM)],
            scratch_shapes=[
                pltpu.VMEM((count, frame, width), jnp.bfloat16),
                pltpu.VMEM((width // PANEL, PANEL), jnp.int32),
                pltpu.VMEM(taps.shape, jnp.float32),
                pltpu.VMEM(table.shape, jnp.bfloat16),
                pltpu.VMEM((width, half), jnp.bfloat16),
                pltpu.VMEM((count, frame, half), jnp.bfloat16),
                pltpu.VMEM((groups, parts, ROWS, half), jnp.bfloat16),
                pltpu.SMEM((TAPS * USED + width // PANEL,), jnp.int32),
                pltpu.SemaphoreType.DMA((3 + TAPS,)),
                pltpu.SemaphoreType.DMA((1 + TAPS,)),
            ],
        ),
        out_shape=[
            pltpu.HBM((depth, frame, half), jnp.bfloat16),
            pltpu.HBM((frame, half), jnp.bfloat16),
            pltpu.HBM((groups, parts, ROWS, WIDTH), jnp.bfloat16),
            jax.ShapeDtypeStruct(block_list.shape, jnp.int32),
        ],
        input_output_aliases=aliases,
        compiler_params=pltpu.CompilerParams(vmem_limit_bytes=VMEM),
        cost_estimate=pl.CostEstimate(
            flops=count * frame * width * WIDTH, bytes_accessed=12 << 20, transcendentals=0
        ),
        name="select",
    )(*operands)


def spectra_kernel(earlier, later, up, down, first, last, taps, table, *out):
    groups = out[0].shape[0]
    depth = TAPS - 1
    cols = first.shape[1]

    def spectra(pool):
        for s in range(depth):
            spectrum = jnp.dot(
                table[...],
                filtered_frame(taps, pool[s : s + TAPS], cols),
                preferred_element_type=jnp.float32,
            ).astype(jnp.bfloat16)
            for q, part in enumerate(out):
                for g in range(groups):
                    at = (q * groups + g) * ROWS
                    part[g, s] = spectrum[at : at + ROWS]

    left = pl.program_id(0) < pl.num_programs(0) // 2

    @pl.when(left)
    def _():
        own = [first[...]] + [up[t] for t in range(depth - 1)]
        spectra([earlier[t] for t in range(depth)] + own)

    @pl.when(jnp.logical_not(left))
    def _():
        ends = lax.axis_index("tm") == lax.axis_size("tm") - 1
        own = [down[t] for t in range(1, depth)] + [last[...]]
        own = [jnp.where(ends, jnp.zeros_like(frame), frame) for frame in own]
        spectra(own + [later[t] for t in range(depth)])


def later_spectra(earlier, later, up, down, first, last, taps, table, groups, parts):
    depth = TAPS - 1
    frame = first.shape[0]
    tiles = WIDTH // LANES // 2
    before = pl.BlockSpec((depth, frame, LANES), lambda k: (0, 0, jnp.minimum(k, tiles - 1)))
    after = pl.BlockSpec((depth, frame, LANES), lambda k: (0, 0, jnp.maximum(k - tiles, 0)))
    return pl.pallas_call(
        spectra_kernel,
        grid=(2 * tiles,),
        in_specs=[
            before,
            after,
            before,
            after,
            pl.BlockSpec((frame, LANES), lambda k: (0, jnp.minimum(k, tiles - 1))),
            pl.BlockSpec((frame, LANES), lambda k: (0, jnp.maximum(k - tiles, 0))),
            pl.BlockSpec((TAPS, frame, PANEL), lambda k: (0, 0, 0)),
            pl.BlockSpec((frame, frame), lambda k: (0, 0)),
        ],
        out_specs=[pl.BlockSpec((groups, depth, ROWS, LANES), lambda k: (0, 0, 0, k))] * parts,
        out_shape=[pltpu.HBM((groups, depth, ROWS, WIDTH), jnp.bfloat16)] * parts,
        compiler_params=pltpu.CompilerParams(vmem_limit_bytes=VMEM // 2),
        cost_estimate=pl.CostEstimate(
            flops=200 * depth * frame * frame * WIDTH, bytes_accessed=10 << 20, transcendentals=0
        ),
        name="later_spectra",
    )(earlier, later, *pin(up, down, first, last, taps, table))


def same_frames(rest, n, cols):
    behind = (TAPS - 1) * ROWS
    at = n * 256
    if cols.start < WIDTH // 2:
        return rest[at : at + 256, cols]
    if n == 0:
        return jnp.concatenate(
            [rest[rest.shape[0] - behind :, cols], rest[: 256 - behind, cols]], axis=0
        )
    return rest[at - behind : at + 256 - behind, cols]


def correlate_kernel(scale, part, blocks, first, rest, orders, *refs):
    out, plain, turned, across, made, go = refs[-6:]
    per = ROWS // 2
    lead = first.shape[0] * ROWS // 256
    total = lead + rest.shape[0] // 256
    width = 256 // per
    for n in range(total):
        for k in range(WIDTH // LANES):
            cols = slice(k * LANES, (k + 1) * LANES)
            if n < lead:
                rows = first[n * 256 // ROWS : (n + 1) * 256 // ROWS, part, :, cols]
                rows = rows.reshape(256, LANES)
            else:
                rows = same_frames(rest, n - lead, cols)
            moved = jnp.dot(orders[...], rows, preferred_element_type=jnp.float32)
            moved = moved.astype(jnp.bfloat16)
            for f in range(per):
                at = f * width
                plain[f, n * width : (n + 1) * width, cols] = moved[at : at + width]
                turned[f, n * width : (n + 1) * width, cols] = moved[256 + at : 256 + at + width]

    def sending(f):
        return pltpu.make_async_copy(made.at[f], out.at[:, :, part * per + f], go.at[f])

    @pl.loop(0, per)
    def _(f):
        across[...] = plain[f].T
        for b in range(blocks.shape[1]):
            a, w = (pl.multiple_of(blocks[i, b], PANEL) for i in range(2))
            left = across[pl.ds(a, PANEL), :]
            right = jnp.concatenate(
                [plain[f, :, pl.ds(w, PANEL)], turned[f, :, pl.ds(w, PANEL)]], axis=1
            )
            product = jnp.dot(left, right, preferred_element_type=jnp.float32) * scale
            made[f, b, 0] = product[:, :PANEL]
            made[f, b, 1] = product[:, PANEL:]
        sending(f).start()

    @pl.loop(0, per)
    def _(f):
        sending(f).wait()


def correlate(places, first, rest, orders, part, shape, so_far):
    groups = first.shape[0]
    per = ROWS // 2
    keys = 2 * groups * TAPS
    rest = rest.reshape(-1, WIDTH)
    blocks = shape[0]
    operands = [places, first, rest, *pin(orders)]
    in_specs = [
        pl.BlockSpec(memory_space=pltpu.VMEM),
        pl.BlockSpec(memory_space=pltpu.VMEM),
        pl.BlockSpec(orders.shape, lambda s, blocks: (0, 0)),
    ]
    aliases = {}
    if so_far is not None:
        aliases = {len(operands): 0}
        operands.append(so_far)
        in_specs.append(pl.BlockSpec(memory_space=pl.ANY))
    return pl.pallas_call(
        functools.partial(correlate_kernel, 1.0 / (groups * TAPS), part),
        grid_spec=pltpu.PrefetchScalarGridSpec(
            num_scalar_prefetch=1,
            grid=(1,),
            in_specs=in_specs,
            out_specs=pl.BlockSpec(memory_space=pl.ANY),
            scratch_shapes=[
                pltpu.VMEM((per, keys, WIDTH), jnp.bfloat16),
                pltpu.VMEM((per, keys, WIDTH), jnp.bfloat16),
                pltpu.VMEM((WIDTH, keys), jnp.bfloat16),
                pltpu.VMEM((per, blocks, 2, PANEL, PANEL), jnp.float32),
                pltpu.SemaphoreType.DMA((per,)),
            ],
        ),
        out_shape=pltpu.HBM(shape, jnp.float32),
        input_output_aliases=aliases,
        compiler_params=pltpu.CompilerParams(vmem_limit_bytes=VMEM // 2),
        cost_estimate=pl.CostEstimate(
            flops=4 * per * keys * PANEL * PANEL * blocks,
            bytes_accessed=18 << 20,
            transcendentals=0,
        ),
        name="correlate",
    )(*operands)


def body(voltages, panel_map, block_list):
    groups = lax.axis_size("tm")
    own = CHANNELS // groups
    parts = own * 2 // ROWS
    frames = voltages.reshape(-1, FRAME, voltages.shape[1])
    taps = filter_taps()
    table = dft_table(groups, parts)
    block_list = block_list.T
    half = functools.partial(
        select, block_list=block_list, panel_map=panel_map, frames=frames, taps=taps,
        table=table, groups=groups, parts=parts,
    )
    up, left, first, places = half(0, so_far=None)
    earlier = shifted(up, "tm", 1, False)
    down, right, first, _ = half(1, so_far=first)
    later = shifted(down, "tm", -1, True)
    exchange = functools.partial(
        lax.all_to_all, axis_name="tm", split_axis=0, concat_axis=0, tiled=True
    )
    first = exchange(first)
    rest = later_spectra(earlier, later, up, down, left, right, taps, table, groups, parts)
    rest = [exchange(part) for part in rest]
    shape = (block_list.shape[1], 2, own, PANEL, PANEL)
    out = None
    for q in range(parts):
        out = correlate(places, first, rest[q], row_orders(), q, shape, out)
    return out


def solution(mesh):
    in_specs = (P(("band", "tm"), None), P(), P())
    out_specs = P("band", None, "tm", None, None)
    return jax.shard_map(body, mesh=mesh, in_specs=in_specs, out_specs=out_specs, check_vma=False)
```

```python
import functools

import jax
import jax.numpy as jnp
import numpy as np
from jax import lax
from jax.experimental import pallas as pl
from jax.experimental.pallas import tpu as pltpu
from jax.sharding import PartitionSpec as P

CHANNELS = 256
TAPS = 4
PANEL = 128
USED = 8
FRAME = 2 * CHANNELS
WIDTH = USED * PANEL
ROWS = 16
PLANE = 4
LANES = 256
VMEM = 60 << 20


def pin(*arrays):
    return [pltpu.with_memory_space_constraint(array, pltpu.HBM) for array in arrays]


def shifted(block, axis, distance, around):
    count = lax.axis_size(axis)
    route = [(i, (i + distance) % count) for i in range(count) if around or 0 <= i + distance < count]
    return lax.ppermute(block, axis, route)


def filter_taps():
    length = TAPS * FRAME
    place = np.arange(length, dtype=np.float64)
    middle = (length - 1) / 2.0
    window = 0.5 - 0.5 * np.cos(2.0 * np.pi * (place + 0.5) / length)
    shape_h = np.sinc((place - middle) / FRAME) * window
    shape_h = shape_h / np.sqrt(np.sum(shape_h * shape_h))
    taps = shape_h.reshape(TAPS, FRAME, 1).astype(np.float32)
    return np.broadcast_to(taps, (TAPS, FRAME, PANEL)).copy()


def dft_table(groups, parts):
    own = CHANNELS // groups
    per = own // parts
    q, g, f, c = np.meshgrid(
        np.arange(parts), np.arange(groups), np.arange(per), np.arange(2), indexing="ij"
    )
    channel = (g * own + q * per + f).reshape(-1)
    imaginary = c.reshape(-1)
    phase = (channel[:, None] * np.arange(FRAME)[None, :] % FRAME) * (2.0 * np.pi / FRAME)
    table = np.where(imaginary[:, None] == 1, -np.sin(phase), np.cos(phase))
    return table.astype(np.float32).astype(jnp.bfloat16)


def row_orders():
    pairs = 256 // ROWS
    half = ROWS // 2
    table = np.zeros((512, 256), np.float32)
    for j in range(pairs):
        for f in range(half):
            row, col = f * pairs * 2 + j * 2, j * ROWS + f * 2
            table[row, col] = 1.0
            table[row + 1, col + 1] = 1.0
            table[256 + row, col + 1] = -1.0
            table[256 + row + 1, col] = 1.0
    return table.astype(jnp.bfloat16)


def named_panels(blocks):
    bits = jnp.int32(0)
    for b in range(blocks.shape[1]):
        bits = bits | (jnp.int32(1) << blocks[0, b])
    return bits


def filtered_frame(taps_ref, frames, cols):
    total = None
    taps = [jnp.tile(taps_ref[t], (1, cols // PANEL)) for t in range(TAPS)]
    for t in range(TAPS):
        term = taps[t] * frames[t].astype(jnp.float32)
        total = term if total is None else total + term
    return total.astype(jnp.bfloat16)


def select_kernel(side, blocks, frames, inputs, *refs):
    halo, hot_out, places, volts, names, hot, chosen, panels, come, go = refs
    depth = TAPS - 1
    order = [(t + 1 - side) % TAPS for t in range(depth)]
    listed = pltpu.make_async_copy(inputs, names, come.at[depth])
    listed.start()
    arrive = [pltpu.make_async_copy(frames.at[t], volts.at[k], come.at[k]) for k, t in enumerate(order)]
    for copy in arrive:
        copy.start()
    bits = named_panels(blocks)
    slot = jnp.int32(0)
    slots = TAPS * USED
    for p in range(inputs.shape[0]):
        panels[slot] = p
        panels[slots + p] = slot * PANEL
        slot = slot + ((bits >> p) & 1)
    listed.wait()
    for j in range(USED // 2):
        wanted = names[pl.ds(panels[side * USED // 2 + j], 1), :]
        rows = lax.broadcasted_iota(jnp.int32, (volts.shape[2], PANEL), 0)
        hot[:, j * PANEL : (j + 1) * PANEL] = (
            (rows == wanted).astype(jnp.float32).astype(jnp.bfloat16)
        )
    sends = []

    def send(source, target):
        sends.append(pltpu.make_async_copy(source, target, go.at[len(sends)]))
        sends[-1].start()

    send(hot, hot_out)
    for k in range(depth):
        arrive[k].wait()
        chosen[k] = jnp.dot(volts[k], hot[...], preferred_element_type=jnp.float32).astype(
            jnp.bfloat16
        )
        send(chosen.at[k], halo.at[k])
    for i in range(2):
        for b in range(blocks.shape[1]):
            places[i, b] = panels[slots + blocks[i, b]]
    for copy in sends:
        copy.wait()


def select(side, block_list, panel_map, frames):
    count, frame, width = frames.shape
    depth = TAPS - 1
    half = WIDTH // 2
    anywhere = pl.BlockSpec(memory_space=pl.ANY)
    return pl.pallas_call(
        functools.partial(select_kernel, side),
        grid_spec=pltpu.PrefetchScalarGridSpec(
            num_scalar_prefetch=1,
            grid=(1,),
            in_specs=[anywhere] * 2,
            out_specs=[anywhere] * 2 + [pl.BlockSpec(memory_space=pltpu.SMEM)],
            scratch_shapes=[
                pltpu.VMEM((depth, frame, width), jnp.bfloat16),
                pltpu.VMEM((width // PANEL, PANEL), jnp.int32),
                pltpu.VMEM((width, half), jnp.bfloat16),
                pltpu.VMEM((depth, frame, half), jnp.bfloat16),
                pltpu.SMEM((TAPS * USED + width // PANEL,), jnp.int32),
                pltpu.SemaphoreType.DMA((TAPS,)),
                pltpu.SemaphoreType.DMA((TAPS,)),
            ],
        ),
        out_shape=[
            pltpu.HBM((depth, frame, half), jnp.bfloat16),
            pltpu.HBM((width, half), jnp.bfloat16),
            jax.ShapeDtypeStruct(block_list.shape, jnp.int32),
        ],
        compiler_params=pltpu.CompilerParams(vmem_limit_bytes=VMEM),
        cost_estimate=pl.CostEstimate(
            flops=depth * frame * width * WIDTH, bytes_accessed=10 << 20, transcendentals=0
        ),
        name="select",
    )(block_list, *pin(frames, panel_map.reshape(-1, PANEL)))


def first_kernel(count, frames, hot0, hot1, up, down, taps, table, *refs):
    kept_out, planes = refs[:2], refs[2 : 2 + count]
    volts, hots, held, kept, spectra, weights, matrix, come, go = refs[2 + count :]
    groups, parts = spectra.shape[0], spectra.shape[1]
    half = WIDTH // 2
    arrive = []

    def fetch(source, target):
        arrive.append(pltpu.make_async_copy(source, target, come.at[len(arrive)]))
        arrive[-1].start()

    for side, (hot, halo) in enumerate(((hot0, up), (hot1, down))):
        fetch(hot, hots.at[side])
        fetch(frames.at[side * (TAPS - 1)], volts.at[side])
        fetch(halo, held.at[side])
        if side == 0:
            fetch(taps, weights)
            fetch(table, matrix)
    sends = []

    def send(source, target):
        sends.append(pltpu.make_async_copy(source, target, go.at[len(sends)]))
        sends[-1].start()

    for side in range(2):
        for copy in arrive[5 * side : 5 * side + 2]:
            copy.wait()
        kept[side] = jnp.dot(
            volts[side], hots[side], preferred_element_type=jnp.float32
        ).astype(jnp.bfloat16)
        send(kept.at[side], kept_out[side])
        for copy in arrive[5 * side + 2 : 5 * side + 5]:
            copy.wait()
        for k in range(half // LANES):
            cols = slice(k * LANES, (k + 1) * LANES)
            pool = [held[side, t, :, cols] for t in range(TAPS - 1)]
            pool.insert(side * (TAPS - 1), kept[side, :, cols])
            spectrum = jnp.dot(
                matrix[...],
                filtered_frame(weights, pool, LANES),
                preferred_element_type=jnp.float32,
            ).astype(jnp.bfloat16)
            at_cols = slice(side * half + k * LANES, side * half + (k + 1) * LANES)
            for q in range(parts):
                for g in range(groups):
                    at = (q * groups + g) * ROWS
                    spectra[g, q, :, at_cols] = spectrum[at : at + ROWS]
    mine = lax.axis_index("tm") // PLANE
    for r, plane in enumerate(planes):
        send(spectra.at[pl.ds((mine ^ r) * PLANE, PLANE)], plane)
    for copy in sends:
        copy.wait()


def first_spectra(frames, hots, up, down, taps, table, groups, parts):
    count, frame, width = frames.shape
    depth = TAPS - 1
    half = WIDTH // 2
    planes = groups // PLANE
    anywhere = pl.BlockSpec(memory_space=pl.ANY)
    return pl.pallas_call(
        functools.partial(first_kernel, planes),
        in_specs=[anywhere] * 7,
        out_specs=[anywhere] * (2 + planes),
        scratch_shapes=[
            pltpu.VMEM((2, frame, width), jnp.bfloat16),
            pltpu.VMEM((2, width, half), jnp.bfloat16),
            pltpu.VMEM((2, depth, frame, half), jnp.bfloat16),
            pltpu.VMEM((2, frame, half), jnp.bfloat16),
            pltpu.VMEM((groups, parts, ROWS, WIDTH), jnp.bfloat16),
            pltpu.VMEM(taps.shape, jnp.float32),
            pltpu.VMEM(table.shape, jnp.bfloat16),
            pltpu.SemaphoreType.DMA((8,)),
            pltpu.SemaphoreType.DMA((2 + planes,)),
        ],
        out_shape=[pltpu.HBM((frame, half), jnp.bfloat16)] * 2
        + [pltpu.HBM((PLANE, parts, ROWS, WIDTH), jnp.bfloat16)] * planes,
        compiler_params=pltpu.CompilerParams(vmem_limit_bytes=VMEM),
        cost_estimate=pl.CostEstimate(
            flops=2 * frame * (width + frame) * WIDTH, bytes_accessed=16 << 20, transcendentals=0
        ),
        name="first_spectra",
    )(*pin(frames, *hots, up, down, taps, table))


def regroup_kernel(*refs):
    planes = len(refs) - 3 - PLANE
    came, left, (held, come, go) = refs[:planes], refs[planes:-3], refs[-3:]
    mine = lax.axis_index("tm") % PLANE
    arrive = [
        [
            pltpu.make_async_copy(plane.at[mine ^ q], held.at[q, r], come.at[q, r])
            for r, plane in enumerate(came)
        ]
        for q in range(PLANE)
    ]
    leave = [pltpu.make_async_copy(held.at[q], left[q], go.at[q]) for q in range(PLANE)]
    for copies in arrive:
        for copy in copies:
            copy.start()
    for copies, copy in zip(arrive, leave):
        for part in copies:
            part.wait()
        copy.start()
    for copy in leave:
        copy.wait()


def regroup(came):
    planes = len(came)
    shape = (planes, *came[0].shape[1:])
    anywhere = pl.BlockSpec(memory_space=pl.ANY)
    return pl.pallas_call(
        regroup_kernel,
        in_specs=[anywhere] * planes,
        out_specs=[anywhere] * PLANE,
        scratch_shapes=[
            pltpu.VMEM((PLANE, *shape), jnp.bfloat16),
            pltpu.SemaphoreType.DMA((PLANE, planes)),
            pltpu.SemaphoreType.DMA((PLANE,)),
        ],
        out_shape=[pltpu.HBM(shape, jnp.bfloat16)] * PLANE,
        cost_estimate=pl.CostEstimate(flops=0, bytes_accessed=2 << 20, transcendentals=0),
        name="regroup",
    )(*came)


def across_planes(planes):
    count = len(planes) * PLANE
    return [planes[0]] + [
        lax.ppermute(plane, "tm", [(i, i ^ (r * PLANE)) for i in range(count)])
        for r, plane in enumerate(planes)
        if r
    ]


def within_plane(came):
    count = len(came) * PLANE
    left = regroup(came)
    return [left[0]] + [
        lax.ppermute(block, "tm", [(i, i ^ q) for i in range(count)])
        for q, block in enumerate(left)
        if q
    ]


def spectra_kernel(side, halo, own, kept, taps, table, *refs):
    out = refs[-1]
    groups, parts = out.shape[0], out.shape[2]
    depth = TAPS - 1
    halos = [halo[t] for t in range(depth)]
    if side:
        ends = lax.axis_index("tm") == lax.axis_size("tm") - 1
        frames = [own[t] for t in range(1, depth)] + [kept[...]]
        pool = [jnp.where(ends, jnp.zeros_like(frame), frame) for frame in frames] + halos
    else:
        pool = halos + [kept[...]] + [own[t] for t in range(depth - 1)]
    for s in range(depth):
        spectrum = jnp.dot(
            table[...],
            filtered_frame(taps, pool[s : s + TAPS], kept.shape[1]),
            preferred_element_type=jnp.float32,
        ).astype(jnp.bfloat16)
        for q in range(parts):
            for g in range(groups):
                at = (q * groups + g) * ROWS
                out[g, s, q] = spectrum[at : at + ROWS]


def later_spectra(side, halo, own, kept, taps, table, groups, parts, so_far):
    depth = TAPS - 1
    frame, cols = kept.shape
    three = pl.BlockSpec((depth, frame, LANES), lambda k: (0, 0, k))
    tiles = cols // LANES
    more = [] if so_far is None else [so_far]
    return pl.pallas_call(
        functools.partial(spectra_kernel, side),
        grid=(cols // LANES,),
        in_specs=[
            three,
            three,
            pl.BlockSpec((frame, LANES), lambda k: (0, k)),
            pl.BlockSpec((TAPS, frame, PANEL), lambda k: (0, 0, 0)),
            pl.BlockSpec((frame, frame), lambda k: (0, 0)),
        ]
        + [pl.BlockSpec(memory_space=pl.ANY)] * len(more),
        out_specs=pl.BlockSpec(
            (groups, depth, parts, ROWS, LANES), lambda k: (0, 0, 0, 0, side * tiles + k)
        ),
        out_shape=pltpu.HBM((groups, depth, parts, ROWS, WIDTH), jnp.bfloat16),
        input_output_aliases={5: 0} if more else {},
        compiler_params=pltpu.CompilerParams(vmem_limit_bytes=VMEM // 2),
        cost_estimate=pl.CostEstimate(
            flops=200 * depth * frame * frame * cols, bytes_accessed=6 << 20, transcendentals=0
        ),
        name="later_spectra",
    )(halo, *pin(own, kept, taps, table), *more)


def correlate_kernel(scale, blocks, *refs):
    sources, rest, orders = refs[:PLANE], refs[PLANE], refs[PLANE + 1]
    out, plain, turned, across, made, first, go, come = refs[-8:]
    groups, depth, parts = rest.shape[0], rest.shape[1], rest.shape[2]
    half = WIDTH // 2
    per = ROWS // 2
    pairs = 256 // ROWS
    width = 256 // per
    arrive = [
        pltpu.make_async_copy(source, first.at[q], come.at[q]) for q, source in enumerate(sources)
    ]
    for copy in arrive:
        copy.start()
    here = [(q, r) for q in range(PLANE) for r in range(groups // PLANE)]
    there = [(g, t) for g in range(groups) for t in range(depth)]
    lead = len(here) // pairs
    total = lead + len(there) // pairs

    def sending(part, f):
        return pltpu.make_async_copy(
            made.at[part, f], out.at[:, :, part * per + f], go.at[part, f]
        )

    for part in range(parts):
        for n in list(range(lead, total)) + list(range(lead)):
            if n == 0 and part == 0:
                for copy in arrive:
                    copy.wait()
            for k in range(WIDTH // LANES):
                cols = slice(k * LANES, (k + 1) * LANES)
                if n < lead:
                    rows = [
                        first[q, r, part, :, cols] for q, r in here[n * pairs : (n + 1) * pairs]
                    ]
                else:
                    some = there[(n - lead) * pairs : (n - lead + 1) * pairs]
                    behind = int(cols.start >= half)
                    rows = [rest[(g - behind) % groups, t, part, :, cols] for g, t in some]
                moved = jnp.dot(
                    orders[...], jnp.concatenate(rows, axis=0), preferred_element_type=jnp.float32
                ).astype(jnp.bfloat16)
                for f in range(per):
                    at = f * width
                    plain[f, n * width : (n + 1) * width, cols] = moved[at : at + width]
                    turned[f, n * width : (n + 1) * width, cols] = moved[
                        256 + at : 256 + at + width
                    ]

        @pl.loop(0, per)
        def _(f):
            across[...] = plain[f].T
            for b in range(blocks.shape[1]):
                a, w = (pl.multiple_of(blocks[i, b], PANEL) for i in range(2))
                product = jnp.dot(
                    across[pl.ds(a, PANEL), :],
                    jnp.concatenate(
                        [plain[f, :, pl.ds(w, PANEL)], turned[f, :, pl.ds(w, PANEL)]], axis=1
                    ),
                    preferred_element_type=jnp.float32,
                )
                made[part, f, b, 0] = product[:, :PANEL] * scale
                made[part, f, b, 1] = product[:, PANEL:] * scale
            sending(part, f).start()

    for part in range(parts):

        @pl.loop(0, per)
        def _(f):
            sending(part, f).wait()


def correlate(places, first, rest, orders, blocks):
    groups, depth, parts = rest.shape[0], rest.shape[1], rest.shape[2]
    per = ROWS // 2
    keys = 2 * groups * TAPS
    shape = (blocks, 2, parts * per, PANEL, PANEL)
    anywhere = pl.BlockSpec(memory_space=pl.ANY)
    inside = pl.BlockSpec(memory_space=pltpu.VMEM)
    return pl.pallas_call(
        functools.partial(correlate_kernel, 1.0 / (groups * TAPS)),
        grid_spec=pltpu.PrefetchScalarGridSpec(
            num_scalar_prefetch=1,
            grid=(1,),
            in_specs=[anywhere] * PLANE
            + [inside, pl.BlockSpec(orders.shape, lambda s, blocks: (0, 0))],
            out_specs=anywhere,
            scratch_shapes=[
                pltpu.VMEM((per, keys, WIDTH), jnp.bfloat16),
                pltpu.VMEM((per, keys, WIDTH), jnp.bfloat16),
                pltpu.VMEM((WIDTH, keys), jnp.bfloat16),
                pltpu.VMEM((parts, per, blocks, 2, PANEL, PANEL), jnp.float32),
                pltpu.VMEM((PLANE, *first[0].shape), jnp.bfloat16),
                pltpu.SemaphoreType.DMA((parts, per)),
                pltpu.SemaphoreType.DMA((PLANE,)),
            ],
        ),
        out_shape=pltpu.HBM(shape, jnp.float32),
        compiler_params=pltpu.CompilerParams(vmem_limit_bytes=VMEM * 5 // 6),
        cost_estimate=pl.CostEstimate(
            flops=4 * parts * per * keys * PANEL * PANEL * blocks,
            bytes_accessed=36 << 20,
            transcendentals=0,
        ),
        name="correlate",
    )(places, *pin(*first), rest, *pin(orders))


def body(voltages, panel_map, block_list):
    groups = lax.axis_size("tm")
    own = CHANNELS // groups
    parts = own * 2 // ROWS
    frames = voltages.reshape(-1, FRAME, voltages.shape[1])
    taps = filter_taps()
    table = dft_table(groups, parts)
    block_list = block_list.T
    up, hot0, places = select(0, block_list, panel_map, frames)
    earlier = shifted(up, "tm", 1, False)
    down, hot1, _ = select(1, block_list, panel_map, frames)
    later = shifted(down, "tm", -1, True)
    left, right, *planes = first_spectra(
        frames, (hot0, hot1), up, down, taps, table, groups, parts
    )
    came = across_planes(planes)
    later_half = functools.partial(
        later_spectra, taps=taps, table=table, groups=groups, parts=parts
    )
    rest = later_half(0, earlier, up, left, so_far=None)
    rest = later_half(1, later, down, right, so_far=rest)
    rest, came = lax.optimization_barrier((rest, came))
    first = within_plane(came)
    rest = lax.all_to_all(rest, "tm", split_axis=0, concat_axis=0, tiled=True)
    return correlate(places, first, rest, row_orders(), block_list.shape[1])


def solution(mesh):
    in_specs = (P(("band", "tm"), None), P(), P())
    out_specs = P("band", None, "tm", None, None)
    return jax.shard_map(body, mesh=mesh, in_specs=in_specs, out_specs=out_specs, check_vma=False)
```

```python
import functools

import jax
import jax.numpy as jnp
import numpy as np
from jax import lax
from jax.experimental import pallas as pl
from jax.experimental.pallas import tpu as pltpu
from jax.sharding import PartitionSpec as P

CHANNELS = 256
TAPS = 4
PANEL = 128
USED = 8
FRAME = 2 * CHANNELS
WIDTH = USED * PANEL
ROWS = 16
PLANE = 4
LANES = 256
VMEM = 60 << 20


def pin(*arrays):
    return [pltpu.with_memory_space_constraint(array, pltpu.HBM) for array in arrays]


def shifted(block, axis, distance, around):
    count = lax.axis_size(axis)
    route = [(i, (i + distance) % count) for i in range(count) if around or 0 <= i + distance < count]
    return lax.ppermute(block, axis, route)


def filter_taps():
    length = TAPS * FRAME
    place = np.arange(length, dtype=np.float64)
    middle = (length - 1) / 2.0
    window = 0.5 - 0.5 * np.cos(2.0 * np.pi * (place + 0.5) / length)
    shape_h = np.sinc((place - middle) / FRAME) * window
    shape_h = shape_h / np.sqrt(np.sum(shape_h * shape_h))
    taps = shape_h.reshape(TAPS, FRAME, 1).astype(np.float32)
    return np.broadcast_to(taps, (TAPS, FRAME, PANEL)).copy()


def dft_table(groups, parts):
    own = CHANNELS // groups
    per = own // parts
    q, g, f, c = np.meshgrid(
        np.arange(parts), np.arange(groups), np.arange(per), np.arange(2), indexing="ij"
    )
    channel = (g * own + q * per + f).reshape(-1)
    imaginary = c.reshape(-1)
    phase = (channel[:, None] * np.arange(FRAME)[None, :] % FRAME) * (2.0 * np.pi / FRAME)
    table = np.where(imaginary[:, None] == 1, -np.sin(phase), np.cos(phase))
    return table.astype(np.float32).astype(jnp.bfloat16)


def row_orders():
    pairs = 256 // ROWS
    half = ROWS // 2
    table = np.zeros((512, 256), np.float32)
    for j in range(pairs):
        for f in range(half):
            row, col = f * pairs * 2 + j * 2, j * ROWS + f * 2
            table[row, col] = 1.0
            table[row + 1, col + 1] = 1.0
            table[256 + row, col + 1] = -1.0
            table[256 + row + 1, col] = 1.0
    return table.astype(jnp.bfloat16)


def named_panels(blocks):
    bits = jnp.int32(0)
    for b in range(blocks.shape[1]):
        bits = bits | (jnp.int32(1) << blocks[0, b])
    return bits


def filtered_frame(taps_ref, frames, cols):
    total = None
    taps = [jnp.tile(taps_ref[t], (1, cols // PANEL)) for t in range(TAPS)]
    for t in range(TAPS):
        term = taps[t] * frames[t].astype(jnp.float32)
        total = term if total is None else total + term
    return total.astype(jnp.bfloat16)


def choose(side, blocks, names, hot, panels):
    bits = named_panels(blocks)
    slot = jnp.int32(0)
    slots = TAPS * USED
    for p in range(names.shape[0]):
        panels[slot] = p
        panels[slots + p] = slot * PANEL
        slot = slot + ((bits >> p) & 1)
    for j in range(USED // 2):
        wanted = names[pl.ds(panels[side * USED // 2 + j], 1), :]
        rows = lax.broadcasted_iota(jnp.int32, (hot.shape[0], PANEL), 0)
        hot[:, j * PANEL : (j + 1) * PANEL] = (
            (rows == wanted).astype(jnp.float32).astype(jnp.bfloat16)
        )


def left_kernel(blocks, frames, inputs, halo, hot, volts, places, names, panels, come):
    listed = pltpu.make_async_copy(inputs, names, come.at[TAPS])
    listed.start()
    order = list(range(1, TAPS)) + [0]
    arrive = [pltpu.make_async_copy(frames.at[t], volts.at[t], come.at[t]) for t in order]
    for copy in arrive[:-1]:
        copy.start()
    listed.wait()
    choose(0, blocks, names, hot, panels)
    for k in range(TAPS - 1):
        arrive[k].wait()
        if k == 0:
            arrive[-1].start()
        halo[k] = jnp.dot(volts[k + 1], hot[...], preferred_element_type=jnp.float32).astype(
            jnp.bfloat16
        )
    for i in range(2):
        for b in range(blocks.shape[1]):
            places[i, b] = panels[TAPS * USED + blocks[i, b]]
    arrive[TAPS - 1].wait()


def right_kernel(blocks, volts, inputs, halo, hot, names, panels, come):
    listed = pltpu.make_async_copy(inputs, names, come.at[TAPS])
    listed.start()
    listed.wait()
    choose(1, blocks, names, hot, panels)
    for k in range(TAPS - 1):
        halo[k] = jnp.dot(volts[k], hot[...], preferred_element_type=jnp.float32).astype(
            jnp.bfloat16
        )


ANYWHERE = pl.BlockSpec(memory_space=pl.ANY)
INSIDE = pl.BlockSpec(memory_space=pltpu.VMEM)


def select(side, block_list, panel_map, frames):
    count, frame, width = frames.shape
    depth = TAPS - 1
    half = WIDTH // 2
    out_specs = [INSIDE, INSIDE]
    out_shape = [
        pltpu.VMEM((depth, frame, half), jnp.bfloat16),
        pltpu.VMEM((width, half), jnp.bfloat16),
    ]
    if side == 0:
        out_specs += [INSIDE, pl.BlockSpec(memory_space=pltpu.SMEM)]
        out_shape += [
            pltpu.VMEM(frames.shape, jnp.bfloat16),
            jax.ShapeDtypeStruct(block_list.shape, jnp.int32),
        ]
    return pl.pallas_call(
        right_kernel if side else left_kernel,
        grid_spec=pltpu.PrefetchScalarGridSpec(
            num_scalar_prefetch=1,
            grid=(1,),
            in_specs=[INSIDE if side else ANYWHERE, ANYWHERE],
            out_specs=out_specs,
            scratch_shapes=[
                pltpu.VMEM((width // PANEL, PANEL), jnp.int32),
                pltpu.SMEM((TAPS * USED + width // PANEL,), jnp.int32),
                pltpu.SemaphoreType.DMA((1 + TAPS,)),
            ],
        ),
        out_shape=out_shape,
        compiler_params=pltpu.CompilerParams(vmem_limit_bytes=VMEM // 2),
        cost_estimate=pl.CostEstimate(
            flops=depth * frame * width * WIDTH, bytes_accessed=10 << 20, transcendentals=0
        ),
        name="select",
    )(block_list, *([frames] if side else pin(frames)), *pin(panel_map.reshape(-1, PANEL)))


def first_kernel(count, volts, hot0, hot1, up, down, taps, table, orders, *refs):
    kept, held, planes = refs[:2], refs[2:5], refs[5 : 5 + count]
    spectra, come, go = refs[5 + count :]
    weights, matrix, _ = held
    groups, parts = spectra.shape[0], spectra.shape[1]
    half = WIDTH // 2
    arrive = [
        pltpu.make_async_copy(source, target, come.at[i])
        for i, (source, target) in enumerate(zip((taps, table, orders), held))
    ]
    for copy in arrive:
        copy.start()
    for side, (hot, halo) in enumerate(((hot0, up), (hot1, down))):
        kept[side][...] = jnp.dot(
            volts[side * (TAPS - 1)], hot[...], preferred_element_type=jnp.float32
        ).astype(jnp.bfloat16)
        if side == 0:
            for copy in arrive:
                copy.wait()
        for k in range(half // LANES):
            cols = slice(k * LANES, (k + 1) * LANES)
            pool = [halo[t, :, cols] for t in range(TAPS - 1)]
            pool.insert(side * (TAPS - 1), kept[side][:, cols])
            spectrum = jnp.dot(
                matrix[...],
                filtered_frame(weights, pool, LANES),
                preferred_element_type=jnp.float32,
            ).astype(jnp.bfloat16)
            at_cols = slice(side * half + k * LANES, side * half + (k + 1) * LANES)
            for q in range(parts):
                for g in range(groups):
                    at = (q * groups + g) * ROWS
                    spectra[g, q, :, at_cols] = spectrum[at : at + ROWS]
    mine = lax.axis_index("tm") // PLANE
    sends = [
        pltpu.make_async_copy(spectra.at[pl.ds((mine ^ r) * PLANE, PLANE)], plane, go.at[r])
        for r, plane in enumerate(planes)
    ]
    for copy in sends:
        copy.start()
    for copy in sends:
        copy.wait()


def first_spectra(volts, hots, up, down, taps, table, orders, groups, parts):
    count, frame, width = volts.shape
    half = WIDTH // 2
    planes = groups // PLANE
    return pl.pallas_call(
        functools.partial(first_kernel, planes),
        in_specs=[INSIDE] * 5 + [ANYWHERE] * 3,
        out_specs=[INSIDE] * 5 + [ANYWHERE] * planes,
        scratch_shapes=[
            pltpu.VMEM((groups, parts, ROWS, WIDTH), jnp.bfloat16),
            pltpu.SemaphoreType.DMA((3,)),
            pltpu.SemaphoreType.DMA((planes,)),
        ],
        out_shape=[pltpu.VMEM((frame, half), jnp.bfloat16)] * 2
        + [pltpu.VMEM(held.shape, held.dtype) for held in (taps, table, orders)]
        + [pltpu.HBM((PLANE, parts, ROWS, WIDTH), jnp.bfloat16)] * planes,
        compiler_params=pltpu.CompilerParams(vmem_limit_bytes=VMEM // 2),
        cost_estimate=pl.CostEstimate(
            flops=2 * frame * (width + frame) * WIDTH, bytes_accessed=16 << 20, transcendentals=0
        ),
        name="first_spectra",
    )(volts, *hots, up, down, *pin(taps, table, orders))


def regroup_kernel(*refs):
    planes = len(refs) - 3 - PLANE
    came, left, (held, come, go) = refs[:planes], refs[planes:-3], refs[-3:]
    mine = lax.axis_index("tm") % PLANE
    arrive = [
        [
            pltpu.make_async_copy(plane.at[mine ^ q], held.at[q, r], come.at[q, r])
            for r, plane in enumerate(came)
        ]
        for q in range(PLANE)
    ]
    leave = [pltpu.make_async_copy(held.at[q], left[q], go.at[q]) for q in range(PLANE)]
    for copies in arrive:
        for copy in copies:
            copy.start()
    for copies, copy in zip(arrive, leave):
        for part in copies:
            part.wait()
        copy.start()
    for copy in leave:
        copy.wait()


def regroup(came):
    planes = len(came)
    shape = (planes, *came[0].shape[1:])
    anywhere = pl.BlockSpec(memory_space=pl.ANY)
    return pl.pallas_call(
        regroup_kernel,
        in_specs=[anywhere] * planes,
        out_specs=[anywhere] * PLANE,
        scratch_shapes=[
            pltpu.VMEM((PLANE, *shape), jnp.bfloat16),
            pltpu.SemaphoreType.DMA((PLANE, planes)),
            pltpu.SemaphoreType.DMA((PLANE,)),
        ],
        out_shape=[pltpu.HBM(shape, jnp.bfloat16)] * PLANE,
        compiler_params=pltpu.CompilerParams(vmem_limit_bytes=VMEM // 12),
        cost_estimate=pl.CostEstimate(flops=1 << 38, bytes_accessed=2 << 20, transcendentals=0),
        name="regroup",
    )(*came)


def across_planes(planes):
    count = len(planes) * PLANE
    return [planes[0]] + [
        lax.ppermute(plane, "tm", [(i, i ^ (r * PLANE)) for i in range(count)])
        for r, plane in enumerate(planes)
        if r
    ]


def within_plane(came):
    count = len(came) * PLANE
    left = regroup(came)
    return [left[0]] + [
        lax.ppermute(block, "tm", [(i, i ^ q) for i in range(count)])
        for q, block in enumerate(left)
        if q
    ]


def spectra_kernel(side, halo, own, kept, taps, table, *refs):
    out, made, go = refs[-3:]
    groups, parts = out.shape[0], out.shape[2]
    depth = TAPS - 1
    half = WIDTH // 2
    sends = []
    for k in range(half // LANES):
        cols = slice(k * LANES, (k + 1) * LANES)
        halos = [halo[t, :, cols] for t in range(depth)]
        if side:
            ends = lax.axis_index("tm") == lax.axis_size("tm") - 1
            frames = [own[t, :, cols] for t in range(1, depth)] + [kept[:, cols]]
            pool = [jnp.where(ends, jnp.zeros_like(frame), frame) for frame in frames] + halos
        else:
            pool = halos + [kept[:, cols]] + [own[t, :, cols] for t in range(depth - 1)]
        for s in range(depth):
            spectrum = jnp.dot(
                table[...],
                filtered_frame(taps, pool[s : s + TAPS], LANES),
                preferred_element_type=jnp.float32,
            ).astype(jnp.bfloat16)
            for q in range(parts):
                for g in range(groups):
                    at = (q * groups + g) * ROWS
                    made[k, g, s, q] = spectrum[at : at + ROWS]
        to = slice(side * half + k * LANES, side * half + (k + 1) * LANES)
        sends.append(pltpu.make_async_copy(made.at[k], out.at[:, :, :, :, to], go.at[k]))
        sends[-1].start()
    for copy in sends:
        copy.wait()


def later_spectra(side, halo, own, kept, taps, table, groups, parts, so_far):
    depth = TAPS - 1
    frame, cols = kept.shape
    more = [] if so_far is None else [so_far]
    return pl.pallas_call(
        functools.partial(spectra_kernel, side),
        in_specs=[INSIDE] * 5 + [ANYWHERE] * len(more),
        out_specs=ANYWHERE,
        out_shape=pltpu.HBM((groups, depth, parts, ROWS, WIDTH), jnp.bfloat16),
        scratch_shapes=[
            pltpu.VMEM((cols // LANES, groups, depth, parts, ROWS, LANES), jnp.bfloat16),
            pltpu.SemaphoreType.DMA((cols // LANES,)),
        ],
        input_output_aliases={5: 0} if more else {},
        compiler_params=pltpu.CompilerParams(vmem_limit_bytes=VMEM // 3),
        cost_estimate=pl.CostEstimate(
            flops=200 * depth * frame * frame * cols, bytes_accessed=6 << 20, transcendentals=0
        ),
        name="later_spectra",
    )(halo, own, kept, taps, table, *more)


def correlate_kernel(scale, blocks, *refs):
    sources, rest, orders = refs[:PLANE], refs[PLANE], refs[PLANE + 1]
    out, plain, turned, across, made, first, go, come = refs[-8:]
    groups, depth, parts = rest.shape[0], rest.shape[1], rest.shape[2]
    half = WIDTH // 2
    per = ROWS // 2
    pairs = 256 // ROWS
    width = 256 // per
    arrive = [
        pltpu.make_async_copy(source, first.at[q], come.at[q]) for q, source in enumerate(sources)
    ]
    for copy in arrive:
        copy.start()
    here = [(q, r) for q in range(PLANE) for r in range(groups // PLANE)]
    there = [(g, t) for g in range(groups) for t in range(depth)]
    lead = len(here) // pairs
    total = lead + len(there) // pairs

    def sending(part, f):
        return pltpu.make_async_copy(
            made.at[part, f], out.at[:, :, part * per + f], go.at[part, f]
        )

    for part in range(parts):
        for n in list(range(lead, total)) + list(range(lead)):
            if n == 0 and part == 0:
                for copy in arrive:
                    copy.wait()
            for k in range(WIDTH // LANES):
                cols = slice(k * LANES, (k + 1) * LANES)
                if n < lead:
                    rows = [
                        first[q, r, part, :, cols] for q, r in here[n * pairs : (n + 1) * pairs]
                    ]
                else:
                    some = there[(n - lead) * pairs : (n - lead + 1) * pairs]
                    behind = int(cols.start >= half)
                    rows = [rest[(g - behind) % groups, t, part, :, cols] for g, t in some]
                moved = jnp.dot(
                    orders[...], jnp.concatenate(rows, axis=0), preferred_element_type=jnp.float32
                ).astype(jnp.bfloat16)
                for f in range(per):
                    at = f * width
                    plain[f, n * width : (n + 1) * width, cols] = moved[at : at + width]
                    turned[f, n * width : (n + 1) * width, cols] = moved[
                        256 + at : 256 + at + width
                    ]

        @pl.loop(0, per)
        def _(f):
            across[...] = plain[f].T
            for b in range(blocks.shape[1]):
                a, w = (pl.multiple_of(blocks[i, b], PANEL) for i in range(2))
                product = jnp.dot(
                    across[pl.ds(a, PANEL), :],
                    jnp.concatenate(
                        [plain[f, :, pl.ds(w, PANEL)], turned[f, :, pl.ds(w, PANEL)]], axis=1
                    ),
                    preferred_element_type=jnp.float32,
                )
                made[part, f, b, 0] = product[:, :PANEL] * scale
                made[part, f, b, 1] = product[:, PANEL:] * scale
            sending(part, f).start()

    for part in range(parts):

        @pl.loop(0, per)
        def _(f):
            sending(part, f).wait()


def correlate(places, first, rest, orders, blocks):
    groups, depth, parts = rest.shape[0], rest.shape[1], rest.shape[2]
    per = ROWS // 2
    keys = 2 * groups * TAPS
    shape = (blocks, 2, parts * per, PANEL, PANEL)
    anywhere = pl.BlockSpec(memory_space=pl.ANY)
    inside = pl.BlockSpec(memory_space=pltpu.VMEM)
    return pl.pallas_call(
        functools.partial(correlate_kernel, 1.0 / (groups * TAPS)),
        grid_spec=pltpu.PrefetchScalarGridSpec(
            num_scalar_prefetch=1,
            grid=(1,),
            in_specs=[anywhere] * PLANE
            + [inside, inside],
            out_specs=anywhere,
            scratch_shapes=[
                pltpu.VMEM((per, keys, WIDTH), jnp.bfloat16),
                pltpu.VMEM((per, keys, WIDTH), jnp.bfloat16),
                pltpu.VMEM((WIDTH, keys), jnp.bfloat16),
                pltpu.VMEM((parts, per, blocks, 2, PANEL, PANEL), jnp.float32),
                pltpu.VMEM((PLANE, *first[0].shape), jnp.bfloat16),
                pltpu.SemaphoreType.DMA((parts, per)),
                pltpu.SemaphoreType.DMA((PLANE,)),
            ],
        ),
        out_shape=pltpu.HBM(shape, jnp.float32),
        compiler_params=pltpu.CompilerParams(vmem_limit_bytes=VMEM * 5//6),
        cost_estimate=pl.CostEstimate(
            flops=4 * parts * per * keys * PANEL * PANEL * blocks,
            bytes_accessed=36 << 20,
            transcendentals=0,
        ),
        name="correlate",
    )(places, *first, rest, orders)


def body(voltages, panel_map, block_list):
    groups = lax.axis_size("tm")
    own = CHANNELS // groups
    parts = own * 2 // ROWS
    frames = voltages.reshape(-1, FRAME, voltages.shape[1])
    taps = filter_taps()
    table = dft_table(groups, parts)
    block_list = block_list.T
    up, hot0, volts, places = select(0, block_list, panel_map, frames)
    earlier = shifted(up, "tm", 1, False)
    down, hot1 = select(1, block_list, panel_map, volts)
    later = shifted(down, "tm", -1, True)
    left, right, taps, table, orders, *planes = first_spectra(
        volts, (hot0, hot1), up, down, taps, table, row_orders(), groups, parts
    )
    came = across_planes(planes)
    later_half = functools.partial(
        later_spectra, taps=taps, table=table, groups=groups, parts=parts
    )
    rest = later_half(0, earlier, up, left, so_far=None)
    rest = later_half(1, later, down, right, so_far=rest)


    first = within_plane(came)
    rest = lax.all_to_all(rest, "tm", split_axis=0, concat_axis=0, tiled=True)
    return correlate(places, first, rest, orders, block_list.shape[1])


def solution(mesh):
    in_specs = (P(("band", "tm"), None), P(), P())
    out_specs = P("band", None, "tm", None, None)
    return jax.shard_map(body, mesh=mesh, in_specs=in_specs, out_specs=out_specs, check_vma=False)
```

```python
import functools

import jax
import jax.numpy as jnp
import numpy as np
from jax import lax
from jax.experimental import pallas as pl
from jax.experimental.pallas import tpu as pltpu
from jax.sharding import PartitionSpec as P

CHANNELS = 256
TAPS = 4
PANEL = 128
USED = 8
FRAME = 2 * CHANNELS
WIDTH = USED * PANEL
ROWS = 16
PLANE = 4
LANES = 256
VMEM = 60 << 20


def pin(*arrays):
    return [pltpu.with_memory_space_constraint(array, pltpu.HBM) for array in arrays]


def shifted(block, axis, distance, around):
    count = lax.axis_size(axis)
    route = [(i, (i + distance) % count) for i in range(count) if around or 0 <= i + distance < count]
    return lax.ppermute(block, axis, route)


def filter_taps():
    length = TAPS * FRAME
    place = np.arange(length, dtype=np.float64)
    middle = (length - 1) / 2.0
    window = 0.5 - 0.5 * np.cos(2.0 * np.pi * (place + 0.5) / length)
    shape_h = np.sinc((place - middle) / FRAME) * window
    shape_h = shape_h / np.sqrt(np.sum(shape_h * shape_h))
    taps = shape_h.reshape(TAPS, FRAME, 1).astype(np.float32)
    return np.broadcast_to(taps, (TAPS, FRAME, PANEL)).copy()


def dft_table(groups, parts):
    own = CHANNELS // groups
    per = own // parts
    q, g, f, c = np.meshgrid(
        np.arange(parts), np.arange(groups), np.arange(per), np.arange(2), indexing="ij"
    )
    channel = (g * own + q * per + f).reshape(-1)
    imaginary = c.reshape(-1)
    phase = (channel[:, None] * np.arange(FRAME)[None, :] % FRAME) * (2.0 * np.pi / FRAME)
    table = np.where(imaginary[:, None] == 1, -np.sin(phase), np.cos(phase))
    return table.astype(np.float32).astype(jnp.bfloat16)


def row_orders():
    pairs = 256 // ROWS
    half = ROWS // 2
    table = np.zeros((512, 256), np.float32)
    for j in range(pairs):
        for f in range(half):
            row, col = f * pairs * 2 + j * 2, j * ROWS + f * 2
            table[row, col] = 1.0
            table[row + 1, col + 1] = 1.0
            table[256 + row, col + 1] = -1.0
            table[256 + row + 1, col] = 1.0
    return table.astype(jnp.bfloat16)


def named_panels(blocks):
    bits = jnp.int32(0)
    for b in range(blocks.shape[1]):
        bits = bits | (jnp.int32(1) << blocks[0, b])
    return bits


def filtered_frame(taps_ref, frames, cols):
    total = None
    taps = [jnp.tile(taps_ref[t], (1, cols // PANEL)) for t in range(TAPS)]
    for t in range(TAPS):
        term = taps[t] * frames[t].astype(jnp.float32)
        total = term if total is None else total + term
    return total.astype(jnp.bfloat16)


def choose(side, blocks, names, hot, panels):
    bits = named_panels(blocks)
    slot = jnp.int32(0)
    slots = TAPS * USED
    for p in range(names.shape[0]):
        panels[slot] = p
        panels[slots + p] = slot * PANEL
        slot = slot + ((bits >> p) & 1)
    for j in range(USED // 2):
        wanted = names[pl.ds(panels[side * USED // 2 + j], 1), :]
        rows = lax.broadcasted_iota(jnp.int32, (hot.shape[0], PANEL), 0)
        hot[:, j * PANEL : (j + 1) * PANEL] = (
            (rows == wanted).astype(jnp.float32).astype(jnp.bfloat16)
        )


def left_kernel(blocks, frames, inputs, halo, hot, volts, places, names, panels, come):
    listed = pltpu.make_async_copy(inputs, names, come.at[TAPS])
    listed.start()
    order = list(range(1, TAPS)) + [0]
    arrive = [pltpu.make_async_copy(frames.at[t], volts.at[t], come.at[t]) for t in order]
    for copy in arrive[:-1]:
        copy.start()
    listed.wait()
    choose(0, blocks, names, hot, panels)
    for k in range(TAPS - 1):
        arrive[k].wait()
        if k == 0:
            arrive[-1].start()
        halo[k] = jnp.dot(volts[k + 1], hot[...], preferred_element_type=jnp.float32).astype(
            jnp.bfloat16
        )
    for i in range(2):
        for b in range(blocks.shape[1]):
            places[i, b] = panels[TAPS * USED + blocks[i, b]]
    arrive[TAPS - 1].wait()


def right_kernel(blocks, volts, inputs, halo, hot, names, panels, come):
    listed = pltpu.make_async_copy(inputs, names, come.at[TAPS])
    listed.start()
    listed.wait()
    choose(1, blocks, names, hot, panels)
    for k in range(TAPS - 1):
        halo[k] = jnp.dot(volts[k], hot[...], preferred_element_type=jnp.float32).astype(
            jnp.bfloat16
        )


ANYWHERE = pl.BlockSpec(memory_space=pl.ANY)
INSIDE = pl.BlockSpec(memory_space=pltpu.VMEM)


def select(side, block_list, panel_map, frames):
    count, frame, width = frames.shape
    depth = TAPS - 1
    half = WIDTH // 2
    out_specs = [INSIDE, INSIDE]
    out_shape = [
        pltpu.VMEM((depth, frame, half), jnp.bfloat16),
        pltpu.VMEM((width, half), jnp.bfloat16),
    ]
    if side == 0:
        out_specs += [INSIDE, pl.BlockSpec(memory_space=pltpu.SMEM)]
        out_shape += [
            pltpu.VMEM(frames.shape, jnp.bfloat16),
            jax.ShapeDtypeStruct(block_list.shape, jnp.int32),
        ]
    return pl.pallas_call(
        right_kernel if side else left_kernel,
        grid_spec=pltpu.PrefetchScalarGridSpec(
            num_scalar_prefetch=1,
            grid=(1,),
            in_specs=[INSIDE if side else ANYWHERE, ANYWHERE],
            out_specs=out_specs,
            scratch_shapes=[
                pltpu.VMEM((width // PANEL, PANEL), jnp.int32),
                pltpu.SMEM((TAPS * USED + width // PANEL,), jnp.int32),
                pltpu.SemaphoreType.DMA((1 + TAPS,)),
            ],
        ),
        out_shape=out_shape,
        compiler_params=pltpu.CompilerParams(vmem_limit_bytes=VMEM // 2),
        cost_estimate=pl.CostEstimate(
            flops=depth * frame * width * WIDTH, bytes_accessed=10 << 20, transcendentals=0
        ),
        name="select",
    )(block_list, *([frames] if side else pin(frames)), *pin(panel_map.reshape(-1, PANEL)))


def first_kernel(count, volts, hot0, hot1, up, down, taps, table, orders, *refs):
    kept, held, planes = refs[:2], refs[2:5], refs[5 : 5 + count]
    spectra, come, go = refs[5 + count :]
    weights, matrix, _ = held
    groups, parts = spectra.shape[0], spectra.shape[1]
    half = WIDTH // 2
    arrive = [
        pltpu.make_async_copy(source, target, come.at[i])
        for i, (source, target) in enumerate(zip((taps, table, orders), held))
    ]
    for copy in arrive:
        copy.start()
    for side, (hot, halo) in enumerate(((hot0, up), (hot1, down))):
        kept[side][...] = jnp.dot(
            volts[side * (TAPS - 1)], hot[...], preferred_element_type=jnp.float32
        ).astype(jnp.bfloat16)
        if side == 0:
            for copy in arrive:
                copy.wait()
        for k in range(half // LANES):
            cols = slice(k * LANES, (k + 1) * LANES)
            pool = [halo[t, :, cols] for t in range(TAPS - 1)]
            pool.insert(side * (TAPS - 1), kept[side][:, cols])
            spectrum = jnp.dot(
                matrix[...],
                filtered_frame(weights, pool, LANES),
                preferred_element_type=jnp.float32,
            ).astype(jnp.bfloat16)
            at_cols = slice(side * half + k * LANES, side * half + (k + 1) * LANES)
            for q in range(parts):
                for g in range(groups):
                    at = (q * groups + g) * ROWS
                    spectra[g, q, :, at_cols] = spectrum[at : at + ROWS]
    mine = lax.axis_index("tm") // PLANE
    sends = [
        pltpu.make_async_copy(spectra.at[pl.ds((mine ^ r) * PLANE, PLANE)], plane, go.at[r])
        for r, plane in enumerate(planes)
    ]
    for copy in sends:
        copy.start()
    for copy in sends:
        copy.wait()


def first_spectra(volts, hots, up, down, taps, table, orders, groups, parts):
    count, frame, width = volts.shape
    half = WIDTH // 2
    planes = groups // PLANE
    return pl.pallas_call(
        functools.partial(first_kernel, planes),
        in_specs=[INSIDE] * 5 + [ANYWHERE] * 3,
        out_specs=[INSIDE] * 5 + [ANYWHERE] * planes,
        scratch_shapes=[
            pltpu.VMEM((groups, parts, ROWS, WIDTH), jnp.bfloat16),
            pltpu.SemaphoreType.DMA((3,)),
            pltpu.SemaphoreType.DMA((planes,)),
        ],
        out_shape=[pltpu.VMEM((frame, half), jnp.bfloat16)] * 2
        + [pltpu.VMEM(held.shape, held.dtype) for held in (taps, table, orders)]
        + [pltpu.HBM((PLANE, parts, ROWS, WIDTH), jnp.bfloat16)] * planes,
        compiler_params=pltpu.CompilerParams(vmem_limit_bytes=VMEM // 2),
        cost_estimate=pl.CostEstimate(
            flops=2 * frame * (width + frame) * WIDTH, bytes_accessed=16 << 20, transcendentals=0
        ),
        name="first_spectra",
    )(volts, *hots, up, down, *pin(taps, table, orders))


def regroup_kernel(*refs):
    planes = len(refs) - 3 - PLANE
    came, left, (held, come, go) = refs[:planes], refs[planes:-3], refs[-3:]
    mine = lax.axis_index("tm") % PLANE
    arrive = [
        [
            pltpu.make_async_copy(plane.at[mine ^ q], held.at[q, r], come.at[q, r])
            for r, plane in enumerate(came)
        ]
        for q in range(PLANE)
    ]
    leave = [pltpu.make_async_copy(held.at[q], left[q], go.at[q]) for q in range(PLANE)]
    for copies in arrive:
        for copy in copies:
            copy.start()
    for copies, copy in zip(arrive, leave):
        for part in copies:
            part.wait()
        copy.start()
    for copy in leave:
        copy.wait()


def regroup(came):
    planes = len(came)
    shape = (planes, *came[0].shape[1:])
    anywhere = pl.BlockSpec(memory_space=pl.ANY)
    return pl.pallas_call(
        regroup_kernel,
        in_specs=[anywhere] * planes,
        out_specs=[anywhere] * PLANE,
        scratch_shapes=[
            pltpu.VMEM((PLANE, *shape), jnp.bfloat16),
            pltpu.SemaphoreType.DMA((PLANE, planes)),
            pltpu.SemaphoreType.DMA((PLANE,)),
        ],
        out_shape=[pltpu.HBM(shape, jnp.bfloat16)] * PLANE,
        compiler_params=pltpu.CompilerParams(vmem_limit_bytes=VMEM // 12),
        cost_estimate=pl.CostEstimate(flops=1 << 37, bytes_accessed=2 << 20, transcendentals=0),
        name="regroup",
    )(*came)


def across_planes(planes):
    count = len(planes) * PLANE
    return [planes[0]] + [
        lax.ppermute(plane, "tm", [(i, i ^ (r * PLANE)) for i in range(count)])
        for r, plane in enumerate(planes)
        if r
    ]


def within_plane(came):
    count = len(came) * PLANE
    left = regroup(came)
    return [left[0]] + [
        lax.ppermute(block, "tm", [(i, i ^ q) for i in range(count)])
        for q, block in enumerate(left)
        if q
    ]


def spectra_kernel(side, halo, own, kept, taps, table, *refs):
    out, made, go = refs[-3:]
    groups, parts = out.shape[0], out.shape[2]
    depth = TAPS - 1
    half = WIDTH // 2
    sends = []
    for k in range(half // LANES):
        cols = slice(k * LANES, (k + 1) * LANES)
        halos = [halo[t, :, cols] for t in range(depth)]
        if side:
            ends = lax.axis_index("tm") == lax.axis_size("tm") - 1
            frames = [own[t, :, cols] for t in range(1, depth)] + [kept[:, cols]]
            pool = [jnp.where(ends, jnp.zeros_like(frame), frame) for frame in frames] + halos
        else:
            pool = halos + [kept[:, cols]] + [own[t, :, cols] for t in range(depth - 1)]
        for s in range(depth):
            spectrum = jnp.dot(
                table[...],
                filtered_frame(taps, pool[s : s + TAPS], LANES),
                preferred_element_type=jnp.float32,
            ).astype(jnp.bfloat16)
            for q in range(parts):
                for g in range(groups):
                    at = (q * groups + g) * ROWS
                    made[k, g, s, q] = spectrum[at : at + ROWS]
        to = slice(side * half + k * LANES, side * half + (k + 1) * LANES)
        sends.append(pltpu.make_async_copy(made.at[k], out.at[:, :, :, :, to], go.at[k]))
        sends[-1].start()
    for copy in sends:
        copy.wait()


def later_spectra(side, halo, own, kept, taps, table, groups, parts, so_far):
    depth = TAPS - 1
    frame, cols = kept.shape
    more = [] if so_far is None else [so_far]
    return pl.pallas_call(
        functools.partial(spectra_kernel, side),
        in_specs=[INSIDE] * 5 + [ANYWHERE] * len(more),
        out_specs=ANYWHERE,
        out_shape=pltpu.HBM((groups, depth, parts, ROWS, WIDTH), jnp.bfloat16),
        scratch_shapes=[
            pltpu.VMEM((cols // LANES, groups, depth, parts, ROWS, LANES), jnp.bfloat16),
            pltpu.SemaphoreType.DMA((cols // LANES,)),
        ],
        input_output_aliases={5: 0} if more else {},
        compiler_params=pltpu.CompilerParams(vmem_limit_bytes=VMEM // 6),
        cost_estimate=pl.CostEstimate(
            flops=200 * depth * frame * frame * cols, bytes_accessed=6 << 20, transcendentals=0
        ),
        name="later_spectra",
    )(halo, own, kept, taps, table, *more)


def correlate_kernel(scale, blocks, *refs):
    sources, rest, orders = refs[:PLANE], refs[PLANE], refs[PLANE + 1]
    out, plain, turned, across, made, first, go, come = refs[-8:]
    groups, depth, parts = rest.shape[0], rest.shape[1], rest.shape[2]
    half = WIDTH // 2
    per = ROWS // 2
    pairs = 256 // ROWS
    width = 256 // per
    arrive = [
        pltpu.make_async_copy(source, first.at[q], come.at[q]) for q, source in enumerate(sources)
    ]
    for copy in arrive:
        copy.start()
    here = [(q, r) for q in range(PLANE) for r in range(groups // PLANE)]
    there = [(g, t) for g in range(groups) for t in range(depth)]
    lead = len(here) // pairs
    total = lead + len(there) // pairs

    def sending(part, f):
        return pltpu.make_async_copy(
            made.at[part, f], out.at[:, :, part * per + f], go.at[part, f]
        )

    for part in range(parts):
        for n in list(range(lead, total)) + list(range(lead)):
            if n == 0 and part == 0:
                for copy in arrive:
                    copy.wait()
            for k in range(WIDTH // LANES):
                cols = slice(k * LANES, (k + 1) * LANES)
                if n < lead:
                    rows = [
                        first[q, r, part, :, cols] for q, r in here[n * pairs : (n + 1) * pairs]
                    ]
                else:
                    some = there[(n - lead) * pairs : (n - lead + 1) * pairs]
                    behind = int(cols.start >= half)
                    rows = [rest[(g - behind) % groups, t, part, :, cols] for g, t in some]
                moved = jnp.dot(
                    orders[...], jnp.concatenate(rows, axis=0), preferred_element_type=jnp.float32
                ).astype(jnp.bfloat16)
                for f in range(per):
                    at = f * width
                    plain[f, n * width : (n + 1) * width, cols] = moved[at : at + width]
                    turned[f, n * width : (n + 1) * width, cols] = moved[
                        256 + at : 256 + at + width
                    ]

        @pl.loop(0, per)
        def _(f):
            across[...] = plain[f].T
            for b in range(blocks.shape[1]):
                a, w = (pl.multiple_of(blocks[i, b], PANEL) for i in range(2))
                product = jnp.dot(
                    across[pl.ds(a, PANEL), :],
                    jnp.concatenate(
                        [plain[f, :, pl.ds(w, PANEL)], turned[f, :, pl.ds(w, PANEL)]], axis=1
                    ),
                    preferred_element_type=jnp.float32,
                )
                made[part, f, b, 0] = product[:, :PANEL] * scale
                made[part, f, b, 1] = product[:, PANEL:] * scale
            sending(part, f).start()

    for part in range(parts):

        @pl.loop(0, per)
        def _(f):
            sending(part, f).wait()


def correlate(places, first, rest, orders, blocks):
    groups, depth, parts = rest.shape[0], rest.shape[1], rest.shape[2]
    per = ROWS // 2
    keys = 2 * groups * TAPS
    shape = (blocks, 2, parts * per, PANEL, PANEL)
    anywhere = pl.BlockSpec(memory_space=pl.ANY)
    inside = pl.BlockSpec(memory_space=pltpu.VMEM)
    return pl.pallas_call(
        functools.partial(correlate_kernel, 1.0 / (groups * TAPS)),
        grid_spec=pltpu.PrefetchScalarGridSpec(
            num_scalar_prefetch=1,
            grid=(1,),
            in_specs=[anywhere] * PLANE
            + [inside, inside],
            out_specs=anywhere,
            scratch_shapes=[
                pltpu.VMEM((per, keys, WIDTH), jnp.bfloat16),
                pltpu.VMEM((per, keys, WIDTH), jnp.bfloat16),
                pltpu.VMEM((WIDTH, keys), jnp.bfloat16),
                pltpu.VMEM((parts, per, blocks, 2, PANEL, PANEL), jnp.float32),
                pltpu.VMEM((PLANE, *first[0].shape), jnp.bfloat16),
                pltpu.SemaphoreType.DMA((parts, per)),
                pltpu.SemaphoreType.DMA((PLANE,)),
            ],
        ),
        out_shape=pltpu.HBM(shape, jnp.float32),
        compiler_params=pltpu.CompilerParams(vmem_limit_bytes=VMEM * 5//6),
        cost_estimate=pl.CostEstimate(
            flops=4 * parts * per * keys * PANEL * PANEL * blocks,
            bytes_accessed=36 << 20,
            transcendentals=0,
        ),
        name="correlate",
    )(places, *pin(*first), rest, orders)


def body(voltages, panel_map, block_list):
    groups = lax.axis_size("tm")
    own = CHANNELS // groups
    parts = own * 2 // ROWS
    frames = voltages.reshape(-1, FRAME, voltages.shape[1])
    taps = filter_taps()
    table = dft_table(groups, parts)
    block_list = block_list.T
    up, hot0, volts, places = select(0, block_list, panel_map, frames)
    earlier = shifted(up, "tm", 1, False)
    down, hot1 = select(1, block_list, panel_map, volts)
    later = shifted(down, "tm", -1, True)
    left, right, taps, table, orders, *planes = first_spectra(
        volts, (hot0, hot1), up, down, taps, table, row_orders(), groups, parts
    )
    came = across_planes(planes)
    later_half = functools.partial(
        later_spectra, taps=taps, table=table, groups=groups, parts=parts
    )
    rest = later_half(0, earlier, up, left, so_far=None)
    rest = later_half(1, later, down, right, so_far=rest)


    first = within_plane(came)
    rest = lax.all_to_all(rest, "tm", split_axis=0, concat_axis=0, tiled=True)
    return correlate(places, first, rest, orders, block_list.shape[1])


def solution(mesh):
    in_specs = (P(("band", "tm"), None), P(), P())
    out_specs = P("band", None, "tm", None, None)
    return jax.shard_map(body, mesh=mesh, in_specs=in_specs, out_specs=out_specs, check_vma=False)
```

```python
import functools

import jax
import jax.numpy as jnp
import numpy as np
from jax import lax
from jax.experimental import pallas as pl
from jax.experimental.pallas import tpu as pltpu
from jax.sharding import PartitionSpec as P

CHANNELS = 256
TAPS = 4
PANEL = 128
USED = 8
FRAME = 2 * CHANNELS
WIDTH = USED * PANEL
ROWS = 16
PLANE = 4
LANES = 256
VMEM = 60 << 20


def pin(*arrays):
    return [pltpu.with_memory_space_constraint(array, pltpu.HBM) for array in arrays]


def shifted(block, axis, distance, around):
    count = lax.axis_size(axis)
    route = [(i, (i + distance) % count) for i in range(count) if around or 0 <= i + distance < count]
    return lax.ppermute(block, axis, route)


def filter_taps():
    length = TAPS * FRAME
    place = np.arange(length, dtype=np.float64)
    middle = (length - 1) / 2.0
    window = 0.5 - 0.5 * np.cos(2.0 * np.pi * (place + 0.5) / length)
    shape_h = np.sinc((place - middle) / FRAME) * window
    shape_h = shape_h / np.sqrt(np.sum(shape_h * shape_h))
    taps = shape_h.reshape(TAPS, FRAME, 1).astype(np.float32)
    return np.broadcast_to(taps, (TAPS, FRAME, PANEL)).copy()


def dft_table(groups, parts):
    own = CHANNELS // groups
    per = own // parts
    q, g, f, c = np.meshgrid(
        np.arange(parts), np.arange(groups), np.arange(per), np.arange(2), indexing="ij"
    )
    channel = (g * own + q * per + f).reshape(-1)
    imaginary = c.reshape(-1)
    phase = (channel[:, None] * np.arange(FRAME)[None, :] % FRAME) * (2.0 * np.pi / FRAME)
    table = np.where(imaginary[:, None] == 1, -np.sin(phase), np.cos(phase))
    return table.astype(np.float32).astype(jnp.bfloat16)


def row_orders():
    pairs = 256 // ROWS
    half = ROWS // 2
    table = np.zeros((512, 256), np.float32)
    for j in range(pairs):
        for f in range(half):
            row, col = f * pairs * 2 + j * 2, j * ROWS + f * 2
            table[row, col] = 1.0
            table[row + 1, col + 1] = 1.0
            table[256 + row, col + 1] = -1.0
            table[256 + row + 1, col] = 1.0
    return table.astype(jnp.bfloat16)


def named_panels(blocks):
    bits = jnp.int32(0)
    for b in range(blocks.shape[1]):
        bits = bits | (jnp.int32(1) << blocks[0, b])
    return bits


def filtered_frame(taps_ref, frames, cols):
    total = None
    taps = [jnp.tile(taps_ref[t], (1, cols // PANEL)) for t in range(TAPS)]
    for t in range(TAPS):
        term = taps[t] * frames[t].astype(jnp.float32)
        total = term if total is None else total + term
    return total.astype(jnp.bfloat16)


def choose(side, blocks, names, hot, panels):
    bits = named_panels(blocks)
    slot = jnp.int32(0)
    slots = TAPS * USED
    for p in range(names.shape[0]):
        panels[slot] = p
        panels[slots + p] = slot * PANEL
        slot = slot + ((bits >> p) & 1)
    for j in range(USED // 2):
        wanted = names[pl.ds(panels[side * USED // 2 + j], 1), :]
        rows = lax.broadcasted_iota(jnp.int32, (hot.shape[0], PANEL), 0)
        hot[:, j * PANEL : (j + 1) * PANEL] = (
            (rows == wanted).astype(jnp.float32).astype(jnp.bfloat16)
        )


def left_kernel(listing, frames, inputs, halo, hot, volts, places, names, panels, blocks, come):
    wanted = pltpu.make_async_copy(listing, blocks, come.at[TAPS + 1])
    wanted.start()
    listed = pltpu.make_async_copy(inputs, names, come.at[TAPS])
    listed.start()
    order = list(range(1, TAPS)) + [0]
    arrive = [pltpu.make_async_copy(frames.at[t], volts.at[t], come.at[t]) for t in order]
    for copy in arrive[:-1]:
        copy.start()
    wanted.wait()
    listed.wait()
    choose(0, blocks, names, hot, panels)
    for k in range(TAPS - 1):
        arrive[k].wait()
        if k == 0:
            arrive[-1].start()
        halo[k] = jnp.dot(volts[k + 1], hot[...], preferred_element_type=jnp.float32).astype(
            jnp.bfloat16
        )
    for i in range(2):
        for b in range(blocks.shape[1]):
            places[i, b] = panels[TAPS * USED + blocks[i, b]]
    arrive[TAPS - 1].wait()


def right_kernel(listing, volts, inputs, halo, hot, names, panels, blocks, come):
    wanted = pltpu.make_async_copy(listing, blocks, come.at[TAPS + 1])
    wanted.start()
    listed = pltpu.make_async_copy(inputs, names, come.at[TAPS])
    listed.start()
    wanted.wait()
    listed.wait()
    choose(1, blocks, names, hot, panels)
    for k in range(TAPS - 1):
        halo[k] = jnp.dot(volts[k], hot[...], preferred_element_type=jnp.float32).astype(
            jnp.bfloat16
        )


ANYWHERE = pl.BlockSpec(memory_space=pl.ANY)
INSIDE = pl.BlockSpec(memory_space=pltpu.VMEM)


def select(side, block_list, panel_map, frames):
    count, frame, width = frames.shape
    depth = TAPS - 1
    half = WIDTH // 2
    out_specs = [INSIDE, INSIDE]
    out_shape = [
        pltpu.VMEM((depth, frame, half), jnp.bfloat16),
        pltpu.VMEM((width, half), jnp.bfloat16),
    ]
    if side == 0:
        out_specs += [INSIDE, pl.BlockSpec(memory_space=pltpu.SMEM)]
        out_shape += [
            pltpu.VMEM(frames.shape, jnp.bfloat16),
            jax.ShapeDtypeStruct(block_list.shape, jnp.int32),
        ]
    return pl.pallas_call(
        right_kernel if side else left_kernel,
        in_specs=[ANYWHERE, INSIDE if side else ANYWHERE, ANYWHERE],
        out_specs=out_specs,
        scratch_shapes=[
            pltpu.VMEM((width // PANEL, PANEL), jnp.int32),
            pltpu.SMEM((TAPS * USED + width // PANEL,), jnp.int32),
            pltpu.SMEM(block_list.shape, jnp.int32),
            pltpu.SemaphoreType.DMA((2 + TAPS,)),
        ],
        out_shape=out_shape,
        compiler_params=pltpu.CompilerParams(vmem_limit_bytes=VMEM // 2),
        cost_estimate=pl.CostEstimate(
            flops=depth * frame * width * WIDTH, bytes_accessed=10 << 20, transcendentals=0
        ),
        name="select",
    )(*pin(block_list), *([frames] if side else pin(frames)), *pin(panel_map.reshape(-1, PANEL)))


def first_kernel(count, volts, hot0, hot1, up, down, taps, table, orders, *refs):
    kept, held, planes = refs[:2], refs[2:5], refs[5 : 5 + count]
    spectra, come, go = refs[5 + count :]
    weights, matrix, _ = held
    groups, parts = spectra.shape[0], spectra.shape[1]
    half = WIDTH // 2
    arrive = [
        pltpu.make_async_copy(source, target, come.at[i])
        for i, (source, target) in enumerate(zip((taps, table, orders), held))
    ]
    for copy in arrive:
        copy.start()
    for side, (hot, halo) in enumerate(((hot0, up), (hot1, down))):
        kept[side][...] = jnp.dot(
            volts[side * (TAPS - 1)], hot[...], preferred_element_type=jnp.float32
        ).astype(jnp.bfloat16)
        if side == 0:
            for copy in arrive:
                copy.wait()
        for k in range(half // LANES):
            cols = slice(k * LANES, (k + 1) * LANES)
            pool = [halo[t, :, cols] for t in range(TAPS - 1)]
            pool.insert(side * (TAPS - 1), kept[side][:, cols])
            spectrum = jnp.dot(
                matrix[...],
                filtered_frame(weights, pool, LANES),
                preferred_element_type=jnp.float32,
            ).astype(jnp.bfloat16)
            at_cols = slice(side * half + k * LANES, side * half + (k + 1) * LANES)
            for q in range(parts):
                for g in range(groups):
                    at = (q * groups + g) * ROWS
                    spectra[g, q, :, at_cols] = spectrum[at : at + ROWS]
    mine = lax.axis_index("tm") // PLANE
    sends = [
        pltpu.make_async_copy(spectra.at[pl.ds((mine ^ r) * PLANE, PLANE)], plane, go.at[r])
        for r, plane in enumerate(planes)
    ]
    for copy in sends:
        copy.start()
    for copy in sends:
        copy.wait()


def first_spectra(volts, hots, up, down, taps, table, orders, groups, parts):
    count, frame, width = volts.shape
    half = WIDTH // 2
    planes = groups // PLANE
    return pl.pallas_call(
        functools.partial(first_kernel, planes),
        in_specs=[INSIDE] * 5 + [ANYWHERE] * 3,
        out_specs=[INSIDE] * 5 + [ANYWHERE] * planes,
        scratch_shapes=[
            pltpu.VMEM((groups, parts, ROWS, WIDTH), jnp.bfloat16),
            pltpu.SemaphoreType.DMA((3,)),
            pltpu.SemaphoreType.DMA((planes,)),
        ],
        out_shape=[pltpu.VMEM((frame, half), jnp.bfloat16)] * 2
        + [pltpu.VMEM(held.shape, held.dtype) for held in (taps, table, orders)]
        + [pltpu.HBM((PLANE, parts, ROWS, WIDTH), jnp.bfloat16)] * planes,
        compiler_params=pltpu.CompilerParams(vmem_limit_bytes=VMEM // 2),
        cost_estimate=pl.CostEstimate(
            flops=2 * frame * (width + frame) * WIDTH, bytes_accessed=16 << 20, transcendentals=0
        ),
        name="first_spectra",
    )(volts, *hots, up, down, *pin(taps, table, orders))


def regroup_kernel(*refs):
    planes = len(refs) - 3 - PLANE
    came, left, (held, come, go) = refs[:planes], refs[planes:-3], refs[-3:]
    mine = lax.axis_index("tm") % PLANE
    arrive = [
        [
            pltpu.make_async_copy(plane.at[mine ^ q], held.at[q, r], come.at[q, r])
            for r, plane in enumerate(came)
        ]
        for q in range(PLANE)
    ]
    leave = [pltpu.make_async_copy(held.at[q], left[q], go.at[q]) for q in range(PLANE)]
    for copies in arrive:
        for copy in copies:
            copy.start()
    for copies, copy in zip(arrive, leave):
        for part in copies:
            part.wait()
        copy.start()
    for copy in leave:
        copy.wait()


def regroup(came):
    planes = len(came)
    shape = (planes, *came[0].shape[1:])
    anywhere = pl.BlockSpec(memory_space=pl.ANY)
    return pl.pallas_call(
        regroup_kernel,
        in_specs=[anywhere] * planes,
        out_specs=[anywhere] * PLANE,
        scratch_shapes=[
            pltpu.VMEM((PLANE, *shape), jnp.bfloat16),
            pltpu.SemaphoreType.DMA((PLANE, planes)),
            pltpu.SemaphoreType.DMA((PLANE,)),
        ],
        out_shape=[pltpu.HBM(shape, jnp.bfloat16)] * PLANE,
        compiler_params=pltpu.CompilerParams(vmem_limit_bytes=VMEM // 12),
        cost_estimate=pl.CostEstimate(flops=1 << 37, bytes_accessed=2 << 20, transcendentals=0),
        name="regroup",
    )(*came)


def across_planes(planes):
    count = len(planes) * PLANE
    return [planes[0]] + [
        lax.ppermute(plane, "tm", [(i, i ^ (r * PLANE)) for i in range(count)])
        for r, plane in enumerate(planes)
        if r
    ]


def within_plane(came):
    count = len(came) * PLANE
    left = regroup(came)
    return [left[0]] + [
        lax.ppermute(block, "tm", [(i, i ^ q) for i in range(count)])
        for q, block in enumerate(left)
        if q
    ]


def spectra_kernel(side, halo, own, kept, taps, table, *refs):
    out, made, go = refs[-3:]
    groups, parts = out.shape[0], out.shape[2]
    depth = TAPS - 1
    half = WIDTH // 2
    sends = []
    for k in range(half // LANES):
        cols = slice(k * LANES, (k + 1) * LANES)
        halos = [halo[t, :, cols] for t in range(depth)]
        if side:
            ends = lax.axis_index("tm") == lax.axis_size("tm") - 1
            frames = [own[t, :, cols] for t in range(1, depth)] + [kept[:, cols]]
            pool = [jnp.where(ends, jnp.zeros_like(frame), frame) for frame in frames] + halos
        else:
            pool = halos + [kept[:, cols]] + [own[t, :, cols] for t in range(depth - 1)]
        for s in range(depth):
            spectrum = jnp.dot(
                table[...],
                filtered_frame(taps, pool[s : s + TAPS], LANES),
                preferred_element_type=jnp.float32,
            ).astype(jnp.bfloat16)
            for q in range(parts):
                for g in range(groups):
                    at = (q * groups + g) * ROWS
                    made[k, g, s, q] = spectrum[at : at + ROWS]
        to = slice(side * half + k * LANES, side * half + (k + 1) * LANES)
        sends.append(pltpu.make_async_copy(made.at[k], out.at[:, :, :, :, to], go.at[k]))
        sends[-1].start()
    for copy in sends:
        copy.wait()


def later_spectra(side, halo, own, kept, taps, table, groups, parts, so_far):
    depth = TAPS - 1
    frame, cols = kept.shape
    more = [] if so_far is None else [so_far]
    return pl.pallas_call(
        functools.partial(spectra_kernel, side),
        in_specs=[INSIDE] * 5 + [ANYWHERE] * len(more),
        out_specs=ANYWHERE,
        out_shape=pltpu.HBM((groups, depth, parts, ROWS, WIDTH), jnp.bfloat16),
        scratch_shapes=[
            pltpu.VMEM((cols // LANES, groups, depth, parts, ROWS, LANES), jnp.bfloat16),
            pltpu.SemaphoreType.DMA((cols // LANES,)),
        ],
        input_output_aliases={5: 0} if more else {},
        compiler_params=pltpu.CompilerParams(vmem_limit_bytes=VMEM // 6),
        cost_estimate=pl.CostEstimate(
            flops=200 * depth * frame * frame * cols, bytes_accessed=6 << 20, transcendentals=0
        ),
        name="later_spectra",
    )(halo, own, kept, taps, table, *more)


def correlate_kernel(scale, blocks, *refs):
    sources, rest, orders = refs[:PLANE], refs[PLANE], refs[PLANE + 1]
    out, plain, turned, across, made, first, go, come = refs[-8:]
    groups, depth, parts = rest.shape[0], rest.shape[1], rest.shape[2]
    half = WIDTH // 2
    per = ROWS // 2
    pairs = 256 // ROWS
    width = 256 // per
    arrive = [
        pltpu.make_async_copy(source, first.at[q], come.at[q]) for q, source in enumerate(sources)
    ]
    for copy in arrive:
        copy.start()
    here = [(q, r) for q in range(PLANE) for r in range(groups // PLANE)]
    there = [(g, t) for g in range(groups) for t in range(depth)]
    lead = len(here) // pairs
    total = lead + len(there) // pairs

    def sending(part, f):
        return pltpu.make_async_copy(
            made.at[part, f], out.at[:, :, part * per + f], go.at[part, f]
        )

    for part in range(parts):
        for n in list(range(lead, total)) + list(range(lead)):
            if n == 0 and part == 0:
                for copy in arrive:
                    copy.wait()
            for k in range(WIDTH // LANES):
                cols = slice(k * LANES, (k + 1) * LANES)
                if n < lead:
                    rows = [
                        first[q, r, part, :, cols] for q, r in here[n * pairs : (n + 1) * pairs]
                    ]
                else:
                    some = there[(n - lead) * pairs : (n - lead + 1) * pairs]
                    behind = int(cols.start >= half)
                    rows = [rest[(g - behind) % groups, t, part, :, cols] for g, t in some]
                moved = jnp.dot(
                    orders[...], jnp.concatenate(rows, axis=0), preferred_element_type=jnp.float32
                ).astype(jnp.bfloat16)
                for f in range(per):
                    at = f * width
                    plain[f, n * width : (n + 1) * width, cols] = moved[at : at + width]
                    turned[f, n * width : (n + 1) * width, cols] = moved[
                        256 + at : 256 + at + width
                    ]

        @pl.loop(0, per)
        def _(f):
            across[...] = plain[f].T
            for b in range(blocks.shape[1]):
                a, w = (pl.multiple_of(blocks[i, b], PANEL) for i in range(2))
                product = jnp.dot(
                    across[pl.ds(a, PANEL), :],
                    jnp.concatenate(
                        [plain[f, :, pl.ds(w, PANEL)], turned[f, :, pl.ds(w, PANEL)]], axis=1
                    ),
                    preferred_element_type=jnp.float32,
                )
                made[part, f, b, 0] = product[:, :PANEL] * scale
                made[part, f, b, 1] = product[:, PANEL:] * scale
            sending(part, f).start()

    for part in range(parts):

        @pl.loop(0, per)
        def _(f):
            sending(part, f).wait()


def correlate(places, first, rest, orders, blocks):
    groups, depth, parts = rest.shape[0], rest.shape[1], rest.shape[2]
    per = ROWS // 2
    keys = 2 * groups * TAPS
    shape = (blocks, 2, parts * per, PANEL, PANEL)
    anywhere = pl.BlockSpec(memory_space=pl.ANY)
    inside = pl.BlockSpec(memory_space=pltpu.VMEM)
    return pl.pallas_call(
        functools.partial(correlate_kernel, 1.0 / (groups * TAPS)),
        grid_spec=pltpu.PrefetchScalarGridSpec(
            num_scalar_prefetch=1,
            grid=(1,),
            in_specs=[anywhere] * PLANE
            + [inside, inside],
            out_specs=anywhere,
            scratch_shapes=[
                pltpu.VMEM((per, keys, WIDTH), jnp.bfloat16),
                pltpu.VMEM((per, keys, WIDTH), jnp.bfloat16),
                pltpu.VMEM((WIDTH, keys), jnp.bfloat16),
                pltpu.VMEM((parts, per, blocks, 2, PANEL, PANEL), jnp.float32),
                pltpu.VMEM((PLANE, *first[0].shape), jnp.bfloat16),
                pltpu.SemaphoreType.DMA((parts, per)),
                pltpu.SemaphoreType.DMA((PLANE,)),
            ],
        ),
        out_shape=pltpu.HBM(shape, jnp.float32),
        compiler_params=pltpu.CompilerParams(vmem_limit_bytes=VMEM * 5//6),
        cost_estimate=pl.CostEstimate(
            flops=4 * parts * per * keys * PANEL * PANEL * blocks,
            bytes_accessed=36 << 20,
            transcendentals=0,
        ),
        name="correlate",
    )(places, *pin(*first), rest, orders)


def body(voltages, panel_map, block_list):
    groups = lax.axis_size("tm")
    own = CHANNELS // groups
    parts = own * 2 // ROWS
    frames = voltages.reshape(-1, FRAME, voltages.shape[1])
    taps = filter_taps()
    table = dft_table(groups, parts)
    block_list = block_list.T
    up, hot0, volts, places = select(0, block_list, panel_map, frames)
    earlier = shifted(up, "tm", 1, False)
    down, hot1 = select(1, block_list, panel_map, volts)
    later = shifted(down, "tm", -1, True)
    left, right, taps, table, orders, *planes = first_spectra(
        volts, (hot0, hot1), up, down, taps, table, row_orders(), groups, parts
    )
    came = across_planes(planes)
    later_half = functools.partial(
        later_spectra, taps=taps, table=table, groups=groups, parts=parts
    )
    rest = later_half(0, earlier, up, left, so_far=None)
    rest = later_half(1, later, down, right, so_far=rest)


    first = within_plane(came)
    rest = lax.all_to_all(rest, "tm", split_axis=0, concat_axis=0, tiled=True)
    return correlate(places, first, rest, orders, block_list.shape[1])


def solution(mesh):
    in_specs = (P(("band", "tm"), None), P(), P())
    out_specs = P("band", None, "tm", None, None)
    return jax.shard_map(body, mesh=mesh, in_specs=in_specs, out_specs=out_specs, check_vma=False)
```

```python
import functools

import jax
import jax.numpy as jnp
import numpy as np
from jax import lax
from jax.experimental import pallas as pl
from jax.experimental.pallas import tpu as pltpu
from jax.sharding import PartitionSpec as P

CHANNELS = 256
TAPS = 4
PANEL = 128
USED = 8
FRAME = 2 * CHANNELS
WIDTH = USED * PANEL
ROWS = 16
PLANE = 4
LANES = 256
VMEM = 60 << 20


def pin(*arrays):
    return [pltpu.with_memory_space_constraint(array, pltpu.HBM) for array in arrays]


def shifted(block, axis, distance, around):
    count = lax.axis_size(axis)
    route = [(i, (i + distance) % count) for i in range(count) if around or 0 <= i + distance < count]
    return lax.ppermute(block, axis, route)


def filter_taps():
    length = TAPS * FRAME
    place = np.arange(length, dtype=np.float64)
    middle = (length - 1) / 2.0
    window = 0.5 - 0.5 * np.cos(2.0 * np.pi * (place + 0.5) / length)
    shape_h = np.sinc((place - middle) / FRAME) * window
    shape_h = shape_h / np.sqrt(np.sum(shape_h * shape_h))
    taps = shape_h.reshape(TAPS, FRAME, 1).astype(np.float32)
    return np.broadcast_to(taps, (TAPS, FRAME, PANEL)).copy()


def dft_table(groups, parts):
    own = CHANNELS // groups
    per = own // parts
    q, g, f, c = np.meshgrid(
        np.arange(parts), np.arange(groups), np.arange(per), np.arange(2), indexing="ij"
    )
    channel = (g * own + q * per + f).reshape(-1)
    imaginary = c.reshape(-1)
    phase = (channel[:, None] * np.arange(FRAME)[None, :] % FRAME) * (2.0 * np.pi / FRAME)
    table = np.where(imaginary[:, None] == 1, -np.sin(phase), np.cos(phase))
    return table.astype(np.float32).astype(jnp.bfloat16)


def row_orders():
    pairs = 256 // ROWS
    half = ROWS // 2
    table = np.zeros((512, 256), np.float32)
    for j in range(pairs):
        for f in range(half):
            row, col = f * pairs * 2 + j * 2, j * ROWS + f * 2
            table[row, col] = 1.0
            table[row + 1, col + 1] = 1.0
            table[256 + row, col + 1] = -1.0
            table[256 + row + 1, col] = 1.0
    return table.astype(jnp.bfloat16)


def named_panels(blocks):
    bits = jnp.int32(0)
    for b in range(blocks.shape[1]):
        bits = bits | (jnp.int32(1) << blocks[0, b])
    return bits


def filtered_frame(taps_ref, frames, cols):
    total = None
    taps = [jnp.tile(taps_ref[t], (1, cols // PANEL)) for t in range(TAPS)]
    for t in range(TAPS):
        term = taps[t] * frames[t].astype(jnp.float32)
        total = term if total is None else total + term
    return total.astype(jnp.bfloat16)


def choose(side, blocks, names, hot, panels):
    bits = named_panels(blocks)
    slot = jnp.int32(0)
    slots = TAPS * USED
    for p in range(names.shape[0]):
        panels[slot] = p
        panels[slots + p] = slot * PANEL
        slot = slot + ((bits >> p) & 1)
    for j in range(USED // 2):
        wanted = names[pl.ds(panels[side * USED // 2 + j], 1), :]
        rows = lax.broadcasted_iota(jnp.int32, (hot.shape[0], PANEL), 0)
        hot[:, j * PANEL : (j + 1) * PANEL] = (
            (rows == wanted).astype(jnp.float32).astype(jnp.bfloat16)
        )


def left_kernel(listing, frames, inputs, halo, hot, volts, places, names, panels, blocks, come):
    wanted = pltpu.make_async_copy(listing, blocks, come.at[TAPS + 1])
    wanted.start()
    listed = pltpu.make_async_copy(inputs, names, come.at[TAPS])
    listed.start()
    order = list(range(1, TAPS)) + [0]
    arrive = [pltpu.make_async_copy(frames.at[t], volts.at[t], come.at[t]) for t in order]
    for copy in arrive[:-1]:
        copy.start()
    wanted.wait()
    listed.wait()
    choose(0, blocks, names, hot, panels)
    for k in range(TAPS - 1):
        arrive[k].wait()
        if k == 0:
            arrive[-1].start()
        halo[k] = jnp.dot(volts[k + 1], hot[...], preferred_element_type=jnp.float32).astype(
            jnp.bfloat16
        )
    for i in range(2):
        for b in range(blocks.shape[1]):
            places[i, b] = panels[TAPS * USED + blocks[i, b]]
    arrive[TAPS - 1].wait()


def right_kernel(listing, volts, inputs, halo, hot, names, panels, blocks, come):
    wanted = pltpu.make_async_copy(listing, blocks, come.at[TAPS + 1])
    wanted.start()
    listed = pltpu.make_async_copy(inputs, names, come.at[TAPS])
    listed.start()
    wanted.wait()
    listed.wait()
    choose(1, blocks, names, hot, panels)
    for k in range(TAPS - 1):
        halo[k] = jnp.dot(volts[k], hot[...], preferred_element_type=jnp.float32).astype(
            jnp.bfloat16
        )


ANYWHERE = pl.BlockSpec(memory_space=pl.ANY)
INSIDE = pl.BlockSpec(memory_space=pltpu.VMEM)


def select(side, block_list, panel_map, frames):
    count, frame, width = frames.shape
    depth = TAPS - 1
    half = WIDTH // 2
    out_specs = [INSIDE, INSIDE]
    out_shape = [
        pltpu.VMEM((depth, frame, half), jnp.bfloat16),
        pltpu.VMEM((width, half), jnp.bfloat16),
    ]
    if side == 0:
        out_specs += [INSIDE, pl.BlockSpec(memory_space=pltpu.SMEM)]
        out_shape += [
            pltpu.VMEM(frames.shape, jnp.bfloat16),
            jax.ShapeDtypeStruct(block_list.shape, jnp.int32),
        ]
    return pl.pallas_call(
        right_kernel if side else left_kernel,
        in_specs=[ANYWHERE, INSIDE if side else ANYWHERE, ANYWHERE],
        out_specs=out_specs,
        scratch_shapes=[
            pltpu.VMEM((width // PANEL, PANEL), jnp.int32),
            pltpu.SMEM((TAPS * USED + width // PANEL,), jnp.int32),
            pltpu.SMEM(block_list.shape, jnp.int32),
            pltpu.SemaphoreType.DMA((2 + TAPS,)),
        ],
        out_shape=out_shape,
        compiler_params=pltpu.CompilerParams(vmem_limit_bytes=VMEM // 2),
        cost_estimate=pl.CostEstimate(
            flops=depth * frame * width * WIDTH, bytes_accessed=10 << 20, transcendentals=0
        ),
        name="select",
    )(*pin(block_list), *([frames] if side else pin(frames)), *pin(panel_map.reshape(-1, PANEL)))


def first_kernel(count, volts, hot0, hot1, up, down, taps, table, orders, *refs):
    kept, held, planes = refs[:2], refs[2:5], refs[5 : 5 + count]
    spectra, come, go = refs[5 + count :]
    weights, matrix, _ = held
    groups, parts = spectra.shape[0], spectra.shape[1]
    half = WIDTH // 2
    arrive = [
        pltpu.make_async_copy(source, target, come.at[i])
        for i, (source, target) in enumerate(zip((taps, table, orders), held))
    ]
    for copy in arrive:
        copy.start()
    for side, (hot, halo) in enumerate(((hot0, up), (hot1, down))):
        kept[side][...] = jnp.dot(
            volts[side * (TAPS - 1)], hot[...], preferred_element_type=jnp.float32
        ).astype(jnp.bfloat16)
        if side == 0:
            for copy in arrive:
                copy.wait()
        for k in range(half // LANES):
            cols = slice(k * LANES, (k + 1) * LANES)
            pool = [halo[t, :, cols] for t in range(TAPS - 1)]
            pool.insert(side * (TAPS - 1), kept[side][:, cols])
            spectrum = jnp.dot(
                matrix[...],
                filtered_frame(weights, pool, LANES),
                preferred_element_type=jnp.float32,
            ).astype(jnp.bfloat16)
            at_cols = slice(side * half + k * LANES, side * half + (k + 1) * LANES)
            for q in range(parts):
                for g in range(groups):
                    at = (q * groups + g) * ROWS
                    spectra[g, q, :, at_cols] = spectrum[at : at + ROWS]
    mine = lax.axis_index("tm") // PLANE
    sends = [
        pltpu.make_async_copy(spectra.at[pl.ds((mine ^ r) * PLANE, PLANE)], plane, go.at[r])
        for r, plane in enumerate(planes)
    ]
    for copy in sends:
        copy.start()
    for copy in sends:
        copy.wait()


def first_spectra(volts, hots, up, down, taps, table, orders, groups, parts):
    count, frame, width = volts.shape
    half = WIDTH // 2
    planes = groups // PLANE
    return pl.pallas_call(
        functools.partial(first_kernel, planes),
        in_specs=[INSIDE] * 5 + [ANYWHERE] * 3,
        out_specs=[INSIDE] * 5 + [ANYWHERE] * planes,
        scratch_shapes=[
            pltpu.VMEM((groups, parts, ROWS, WIDTH), jnp.bfloat16),
            pltpu.SemaphoreType.DMA((3,)),
            pltpu.SemaphoreType.DMA((planes,)),
        ],
        out_shape=[pltpu.VMEM((frame, half), jnp.bfloat16)] * 2
        + [pltpu.VMEM(held.shape, held.dtype) for held in (taps, table, orders)]
        + [pltpu.HBM((PLANE, parts, ROWS, WIDTH), jnp.bfloat16)] * planes,
        compiler_params=pltpu.CompilerParams(vmem_limit_bytes=VMEM // 2),
        cost_estimate=pl.CostEstimate(
            flops=2 * frame * (width + frame) * WIDTH, bytes_accessed=16 << 20, transcendentals=0
        ),
        name="first_spectra",
    )(volts, *hots, up, down, *pin(taps, table, orders))


def regroup_kernel(*refs):
    planes = len(refs) - 3 - PLANE
    came, left, (held, come, go) = refs[:planes], refs[planes:-3], refs[-3:]
    mine = lax.axis_index("tm") % PLANE
    arrive = [
        [
            pltpu.make_async_copy(plane.at[mine ^ q], held.at[q, r], come.at[q, r])
            for r, plane in enumerate(came)
        ]
        for q in range(PLANE)
    ]
    leave = [pltpu.make_async_copy(held.at[q], left[q], go.at[q]) for q in range(PLANE)]
    for copies in arrive:
        for copy in copies:
            copy.start()
    for copies, copy in zip(arrive, leave):
        for part in copies:
            part.wait()
        copy.start()
    for copy in leave:
        copy.wait()


def regroup(came):
    planes = len(came)
    shape = (planes, *came[0].shape[1:])
    anywhere = pl.BlockSpec(memory_space=pl.ANY)
    return pl.pallas_call(
        regroup_kernel,
        in_specs=[anywhere] * planes,
        out_specs=[anywhere] * PLANE,
        scratch_shapes=[
            pltpu.VMEM((PLANE, *shape), jnp.bfloat16),
            pltpu.SemaphoreType.DMA((PLANE, planes)),
            pltpu.SemaphoreType.DMA((PLANE,)),
        ],
        out_shape=[pltpu.HBM(shape, jnp.bfloat16)] * PLANE,
        compiler_params=pltpu.CompilerParams(vmem_limit_bytes=VMEM // 12),
        cost_estimate=pl.CostEstimate(flops=1 << 37, bytes_accessed=2 << 20, transcendentals=0),
        name="regroup",
    )(*came)


def across_planes(planes):
    count = len(planes) * PLANE
    return [planes[0]] + [
        lax.ppermute(plane, "tm", [(i, i ^ (r * PLANE)) for i in range(count)])
        for r, plane in enumerate(planes)
        if r
    ]


def within_plane(came):
    count = len(came) * PLANE
    left = regroup(came)
    return [left[0]] + [
        lax.ppermute(block, "tm", [(i, i ^ q) for i in range(count)])
        for q, block in enumerate(left)
        if q
    ]


def spectra_kernel(side, halo, own, kept, taps, table, *refs):
    out, made, go = refs[-3:]
    groups, parts = out.shape[0], out.shape[2]
    depth = TAPS - 1
    half = WIDTH // 2
    sends = []
    for k in range(half // LANES):
        cols = slice(k * LANES, (k + 1) * LANES)
        halos = [halo[t, :, cols] for t in range(depth)]
        if side:
            ends = lax.axis_index("tm") == lax.axis_size("tm") - 1
            frames = [own[t, :, cols] for t in range(1, depth)] + [kept[:, cols]]
            pool = [jnp.where(ends, jnp.zeros_like(frame), frame) for frame in frames] + halos
        else:
            pool = halos + [kept[:, cols]] + [own[t, :, cols] for t in range(depth - 1)]
        for s in range(depth):
            spectrum = jnp.dot(
                table[...],
                filtered_frame(taps, pool[s : s + TAPS], LANES),
                preferred_element_type=jnp.float32,
            ).astype(jnp.bfloat16)
            for q in range(parts):
                for g in range(groups):
                    at = (q * groups + g) * ROWS
                    made[k, g, s, q] = spectrum[at : at + ROWS]
        to = slice(side * half + k * LANES, side * half + (k + 1) * LANES)
        sends.append(pltpu.make_async_copy(made.at[k], out.at[:, :, :, :, to], go.at[k]))
        sends[-1].start()
    for copy in sends:
        copy.wait()


def later_spectra(side, halo, own, kept, taps, table, groups, parts, so_far):
    depth = TAPS - 1
    frame, cols = kept.shape
    more = [] if so_far is None else [so_far]
    return pl.pallas_call(
        functools.partial(spectra_kernel, side),
        in_specs=[INSIDE] * 5 + [ANYWHERE] * len(more),
        out_specs=ANYWHERE,
        out_shape=pltpu.HBM((groups, depth, parts, ROWS, WIDTH), jnp.bfloat16),
        scratch_shapes=[
            pltpu.VMEM((cols // LANES, groups, depth, parts, ROWS, LANES), jnp.bfloat16),
            pltpu.SemaphoreType.DMA((cols // LANES,)),
        ],
        input_output_aliases={5: 0} if more else {},
        compiler_params=pltpu.CompilerParams(vmem_limit_bytes=VMEM // 6),
        cost_estimate=pl.CostEstimate(
            flops=200 * depth * frame * frame * cols, bytes_accessed=6 << 20, transcendentals=0
        ),
        name="later_spectra",
    )(halo, own, kept, taps, table, *more)


def correlate_kernel(scale, blocks, *refs):
    sources, rest, orders = refs[:PLANE], refs[PLANE], refs[PLANE + 1]
    out, plain, turned, across, made, first, go, come = refs[-8:]
    groups, depth, parts = rest.shape[0], rest.shape[1], rest.shape[2]
    half = WIDTH // 2
    per = ROWS // 2
    pairs = 256 // ROWS
    width = 256 // per
    arrive = [
        pltpu.make_async_copy(source, first.at[q], come.at[q]) for q, source in enumerate(sources)
    ]
    for copy in arrive:
        copy.start()
    here = [(q, r) for q in range(PLANE) for r in range(groups // PLANE)]
    there = [(g, t) for g in range(groups) for t in range(depth)]
    lead = len(here) // pairs
    total = lead + len(there) // pairs

    def sending(part, f):
        return pltpu.make_async_copy(
            made.at[part, f], out.at[:, :, part * per + f], go.at[part, f]
        )

    for part in range(parts):
        for n in list(range(lead, total)) + list(range(lead)):
            if n == 0 and part == 0:
                for copy in arrive:
                    copy.wait()
            for k in range(WIDTH // LANES):
                cols = slice(k * LANES, (k + 1) * LANES)
                if n < lead:
                    rows = [
                        first[q, r, part, :, cols] for q, r in here[n * pairs : (n + 1) * pairs]
                    ]
                else:
                    some = there[(n - lead) * pairs : (n - lead + 1) * pairs]
                    behind = int(cols.start >= half)
                    rows = [rest[(g - behind) % groups, t, part, :, cols] for g, t in some]
                moved = jnp.dot(
                    orders[...], jnp.concatenate(rows, axis=0), preferred_element_type=jnp.float32
                ).astype(jnp.bfloat16)
                for f in range(per):
                    at = f * width
                    plain[f, n * width : (n + 1) * width, cols] = moved[at : at + width]
                    turned[f, n * width : (n + 1) * width, cols] = moved[
                        256 + at : 256 + at + width
                    ]

        @pl.loop(0, per, unroll=2)
        def _(f):
            across[f % 2] = plain[f].T
            for b in range(blocks.shape[1]):
                a, w = (pl.multiple_of(blocks[i, b], PANEL) for i in range(2))
                product = jnp.dot(
                    across[f % 2, pl.ds(a, PANEL), :],
                    jnp.concatenate(
                        [plain[f, :, pl.ds(w, PANEL)], turned[f, :, pl.ds(w, PANEL)]], axis=1
                    ),
                    preferred_element_type=jnp.float32,
                )
                made[part, f, b, 0] = product[:, :PANEL] * scale
                made[part, f, b, 1] = product[:, PANEL:] * scale
            sending(part, f).start()

    for part in range(parts):

        @pl.loop(0, per)
        def _(f):
            sending(part, f).wait()


def correlate(places, first, rest, orders, blocks):
    groups, depth, parts = rest.shape[0], rest.shape[1], rest.shape[2]
    per = ROWS // 2
    keys = 2 * groups * TAPS
    shape = (blocks, 2, parts * per, PANEL, PANEL)
    anywhere = pl.BlockSpec(memory_space=pl.ANY)
    inside = pl.BlockSpec(memory_space=pltpu.VMEM)
    return pl.pallas_call(
        functools.partial(correlate_kernel, 1.0 / (groups * TAPS)),
        grid_spec=pltpu.PrefetchScalarGridSpec(
            num_scalar_prefetch=1,
            grid=(1,),
            in_specs=[anywhere] * PLANE
            + [inside, inside],
            out_specs=anywhere,
            scratch_shapes=[
                pltpu.VMEM((per, keys, WIDTH), jnp.bfloat16),
                pltpu.VMEM((per, keys, WIDTH), jnp.bfloat16),
                pltpu.VMEM((2, WIDTH, keys), jnp.bfloat16),
                pltpu.VMEM((parts, per, blocks, 2, PANEL, PANEL), jnp.float32),
                pltpu.VMEM((PLANE, *first[0].shape), jnp.bfloat16),
                pltpu.SemaphoreType.DMA((parts, per)),
                pltpu.SemaphoreType.DMA((PLANE,)),
            ],
        ),
        out_shape=pltpu.HBM(shape, jnp.float32),
        compiler_params=pltpu.CompilerParams(vmem_limit_bytes=VMEM * 5//6),
        cost_estimate=pl.CostEstimate(
            flops=4 * parts * per * keys * PANEL * PANEL * blocks,
            bytes_accessed=36 << 20,
            transcendentals=0,
        ),
        name="correlate",
    )(places, *pin(*first), rest, orders)


def body(voltages, panel_map, block_list):
    groups = lax.axis_size("tm")
    own = CHANNELS // groups
    parts = own * 2 // ROWS
    frames = voltages.reshape(-1, FRAME, voltages.shape[1])
    taps = filter_taps()
    table = dft_table(groups, parts)
    block_list = block_list.T
    up, hot0, volts, places = select(0, block_list, panel_map, frames)
    earlier = shifted(up, "tm", 1, False)
    down, hot1 = select(1, block_list, panel_map, volts)
    later = shifted(down, "tm", -1, True)
    left, right, taps, table, orders, *planes = first_spectra(
        volts, (hot0, hot1), up, down, taps, table, row_orders(), groups, parts
    )
    came = across_planes(planes)
    later_half = functools.partial(
        later_spectra, taps=taps, table=table, groups=groups, parts=parts
    )
    rest = later_half(0, earlier, up, left, so_far=None)
    rest = later_half(1, later, down, right, so_far=rest)


    first = within_plane(came)
    rest = lax.all_to_all(rest, "tm", split_axis=0, concat_axis=0, tiled=True)
    return correlate(places, first, rest, orders, block_list.shape[1])


def solution(mesh):
    in_specs = (P(("band", "tm"), None), P(), P())
    out_specs = P("band", None, "tm", None, None)
    return jax.shard_map(body, mesh=mesh, in_specs=in_specs, out_specs=out_specs, check_vma=False)
```

```python
import functools

import jax
import jax.numpy as jnp
import numpy as np
from jax import lax
from jax.experimental import pallas as pl
from jax.experimental.pallas import tpu as pltpu
from jax.sharding import PartitionSpec as P

CHANNELS = 256
TAPS = 4
PANEL = 128
USED = 8
FRAME = 2 * CHANNELS
WIDTH = USED * PANEL
ROWS = 16
PLANE = 4
LANES = 256
VMEM = 60 << 20


def pin(*arrays):
    return [pltpu.with_memory_space_constraint(array, pltpu.HBM) for array in arrays]


def shifted(block, axis, distance, around):
    count = lax.axis_size(axis)
    route = [(i, (i + distance) % count) for i in range(count) if around or 0 <= i + distance < count]
    return lax.ppermute(block, axis, route)


def filter_taps():
    length = TAPS * FRAME
    place = np.arange(length, dtype=np.float64)
    middle = (length - 1) / 2.0
    window = 0.5 - 0.5 * np.cos(2.0 * np.pi * (place + 0.5) / length)
    shape_h = np.sinc((place - middle) / FRAME) * window
    shape_h = shape_h / np.sqrt(np.sum(shape_h * shape_h))
    taps = shape_h.reshape(TAPS, FRAME, 1).astype(np.float32)
    return np.broadcast_to(taps, (TAPS, FRAME, PANEL)).copy()


def dft_table(groups, parts):
    own = CHANNELS // groups
    per = own // parts
    q, g, f, c = np.meshgrid(
        np.arange(parts), np.arange(groups), np.arange(per), np.arange(2), indexing="ij"
    )
    channel = (g * own + q * per + f).reshape(-1)
    imaginary = c.reshape(-1)
    phase = (channel[:, None] * np.arange(FRAME)[None, :] % FRAME) * (2.0 * np.pi / FRAME)
    table = np.where(imaginary[:, None] == 1, -np.sin(phase), np.cos(phase))
    return table.astype(np.float32).astype(jnp.bfloat16)


def row_orders():
    pairs = 256 // ROWS
    half = ROWS // 2
    table = np.zeros((512, 256), np.float32)
    for j in range(pairs):
        for f in range(half):
            row, col = f * pairs * 2 + j * 2, j * ROWS + f * 2
            table[row, col] = 1.0
            table[row + 1, col + 1] = 1.0
            table[256 + row, col + 1] = -1.0
            table[256 + row + 1, col] = 1.0
    return table.astype(jnp.bfloat16)


def named_panels(blocks):
    bits = jnp.int32(0)
    for b in range(blocks.shape[1]):
        bits = bits | (jnp.int32(1) << blocks[0, b])
    return bits


def filtered_frame(taps_ref, frames, cols):
    total = None
    taps = [jnp.tile(taps_ref[t], (1, cols // PANEL)) for t in range(TAPS)]
    for t in range(TAPS):
        term = taps[t] * frames[t].astype(jnp.float32)
        total = term if total is None else total + term
    return total.astype(jnp.bfloat16)


def choose(side, blocks, names, hot, panels):
    bits = named_panels(blocks)
    slot = jnp.int32(0)
    slots = TAPS * USED
    for p in range(names.shape[0]):
        panels[slot] = p
        panels[slots + p] = slot * PANEL
        slot = slot + ((bits >> p) & 1)
    for j in range(USED // 2):
        wanted = names[pl.ds(panels[side * USED // 2 + j], 1), :]
        rows = lax.broadcasted_iota(jnp.int32, (hot.shape[0], PANEL), 0)
        hot[:, j * PANEL : (j + 1) * PANEL] = (
            (rows == wanted).astype(jnp.float32).astype(jnp.bfloat16)
        )


def left_kernel(listing, frames, inputs, halo, hot, volts, places, names, panels, blocks, come):
    wanted = pltpu.make_async_copy(listing, blocks, come.at[TAPS + 1])
    wanted.start()
    listed = pltpu.make_async_copy(inputs, names, come.at[TAPS])
    listed.start()
    order = list(range(1, TAPS)) + [0]
    arrive = [pltpu.make_async_copy(frames.at[t], volts.at[t], come.at[t]) for t in order]
    for copy in arrive[:-1]:
        copy.start()
    wanted.wait()
    listed.wait()
    choose(0, blocks, names, hot, panels)
    for k in range(TAPS - 1):
        arrive[k].wait()
        if k == 0:
            arrive[-1].start()
        halo[k] = jnp.dot(volts[k + 1], hot[...], preferred_element_type=jnp.float32).astype(
            jnp.bfloat16
        )
    for i in range(2):
        for b in range(blocks.shape[1]):
            places[i, b] = panels[TAPS * USED + blocks[i, b]]
    arrive[TAPS - 1].wait()


def right_kernel(listing, volts, inputs, halo, hot, names, panels, blocks, come):
    wanted = pltpu.make_async_copy(listing, blocks, come.at[TAPS + 1])
    wanted.start()
    listed = pltpu.make_async_copy(inputs, names, come.at[TAPS])
    listed.start()
    wanted.wait()
    listed.wait()
    choose(1, blocks, names, hot, panels)
    for k in range(TAPS - 1):
        halo[k] = jnp.dot(volts[k], hot[...], preferred_element_type=jnp.float32).astype(
            jnp.bfloat16
        )


ANYWHERE = pl.BlockSpec(memory_space=pl.ANY)
INSIDE = pl.BlockSpec(memory_space=pltpu.VMEM)


def select(side, block_list, panel_map, frames):
    count, frame, width = frames.shape
    depth = TAPS - 1
    half = WIDTH // 2
    out_specs = [INSIDE, INSIDE]
    out_shape = [
        pltpu.VMEM((depth, frame, half), jnp.bfloat16),
        pltpu.VMEM((width, half), jnp.bfloat16),
    ]
    if side == 0:
        out_specs += [INSIDE, pl.BlockSpec(memory_space=pltpu.SMEM)]
        out_shape += [
            pltpu.VMEM(frames.shape, jnp.bfloat16),
            jax.ShapeDtypeStruct(block_list.shape, jnp.int32),
        ]
    return pl.pallas_call(
        right_kernel if side else left_kernel,
        in_specs=[ANYWHERE, INSIDE if side else ANYWHERE, ANYWHERE],
        out_specs=out_specs,
        scratch_shapes=[
            pltpu.VMEM((width // PANEL, PANEL), jnp.int32),
            pltpu.SMEM((TAPS * USED + width // PANEL,), jnp.int32),
            pltpu.SMEM(block_list.shape, jnp.int32),
            pltpu.SemaphoreType.DMA((2 + TAPS,)),
        ],
        out_shape=out_shape,
        compiler_params=pltpu.CompilerParams(vmem_limit_bytes=VMEM // 2),
        cost_estimate=pl.CostEstimate(
            flops=depth * frame * width * WIDTH, bytes_accessed=10 << 20, transcendentals=0
        ),
        name="select",
    )(*pin(block_list), *([frames] if side else pin(frames)), *pin(panel_map.reshape(-1, PANEL)))


def first_kernel(count, volts, hot0, hot1, up, down, taps, table, orders, *refs):
    kept, held, planes = refs[:2], refs[2:5], refs[5 : 5 + count]
    spectra, come, go = refs[5 + count :]
    weights, matrix, _ = held
    groups, parts = spectra.shape[0], spectra.shape[1]
    half = WIDTH // 2
    arrive = [
        pltpu.make_async_copy(source, target, come.at[i])
        for i, (source, target) in enumerate(zip((taps, table, orders), held))
    ]
    for copy in arrive:
        copy.start()
    for side, (hot, halo) in enumerate(((hot0, up), (hot1, down))):
        kept[side][...] = jnp.dot(
            volts[side * (TAPS - 1)], hot[...], preferred_element_type=jnp.float32
        ).astype(jnp.bfloat16)
        if side == 0:
            for copy in arrive:
                copy.wait()
        for k in range(half // LANES):
            cols = slice(k * LANES, (k + 1) * LANES)
            pool = [halo[t, :, cols] for t in range(TAPS - 1)]
            pool.insert(side * (TAPS - 1), kept[side][:, cols])
            spectrum = jnp.dot(
                matrix[...],
                filtered_frame(weights, pool, LANES),
                preferred_element_type=jnp.float32,
            ).astype(jnp.bfloat16)
            at_cols = slice(side * half + k * LANES, side * half + (k + 1) * LANES)
            for q in range(parts):
                for g in range(groups):
                    at = (q * groups + g) * ROWS
                    spectra[g, q, :, at_cols] = spectrum[at : at + ROWS]
    mine = lax.axis_index("tm") // PLANE
    sends = [
        pltpu.make_async_copy(spectra.at[pl.ds((mine ^ r) * PLANE, PLANE)], plane, go.at[r])
        for r, plane in enumerate(planes)
    ]
    for copy in sends:
        copy.start()
    for copy in sends:
        copy.wait()


def first_spectra(volts, hots, up, down, taps, table, orders, groups, parts):
    count, frame, width = volts.shape
    half = WIDTH // 2
    planes = groups // PLANE
    return pl.pallas_call(
        functools.partial(first_kernel, planes),
        in_specs=[INSIDE] * 5 + [ANYWHERE] * 3,
        out_specs=[INSIDE] * 5 + [ANYWHERE] * planes,
        scratch_shapes=[
            pltpu.VMEM((groups, parts, ROWS, WIDTH), jnp.bfloat16),
            pltpu.SemaphoreType.DMA((3,)),
            pltpu.SemaphoreType.DMA((planes,)),
        ],
        out_shape=[pltpu.VMEM((frame, half), jnp.bfloat16)] * 2
        + [pltpu.VMEM(held.shape, held.dtype) for held in (taps, table, orders)]
        + [pltpu.HBM((PLANE, parts, ROWS, WIDTH), jnp.bfloat16)] * planes,
        compiler_params=pltpu.CompilerParams(vmem_limit_bytes=VMEM // 2),
        cost_estimate=pl.CostEstimate(
            flops=2 * frame * (width + frame) * WIDTH, bytes_accessed=16 << 20, transcendentals=0
        ),
        name="first_spectra",
    )(volts, *hots, up, down, *pin(taps, table, orders))


def regroup_kernel(*refs):
    planes = len(refs) - 3 - PLANE
    came, left, (held, come, go) = refs[:planes], refs[planes:-3], refs[-3:]
    mine = lax.axis_index("tm") % PLANE
    arrive = [
        [
            pltpu.make_async_copy(plane.at[mine ^ q], held.at[q, r], come.at[q, r])
            for r, plane in enumerate(came)
        ]
        for q in range(PLANE)
    ]
    leave = [pltpu.make_async_copy(held.at[q], left[q], go.at[q]) for q in range(PLANE)]
    for copies in arrive:
        for copy in copies:
            copy.start()
    for copies, copy in zip(arrive, leave):
        for part in copies:
            part.wait()
        copy.start()
    for copy in leave:
        copy.wait()


def regroup(came):
    planes = len(came)
    shape = (planes, *came[0].shape[1:])
    anywhere = pl.BlockSpec(memory_space=pl.ANY)
    return pl.pallas_call(
        regroup_kernel,
        in_specs=[anywhere] * planes,
        out_specs=[anywhere] * PLANE,
        scratch_shapes=[
            pltpu.VMEM((PLANE, *shape), jnp.bfloat16),
            pltpu.SemaphoreType.DMA((PLANE, planes)),
            pltpu.SemaphoreType.DMA((PLANE,)),
        ],
        out_shape=[pltpu.HBM(shape, jnp.bfloat16)] * PLANE,
        compiler_params=pltpu.CompilerParams(vmem_limit_bytes=VMEM // 12),
        cost_estimate=pl.CostEstimate(flops=1 << 37, bytes_accessed=2 << 20, transcendentals=0),
        name="regroup",
    )(*came)


def across_planes(planes):
    count = len(planes) * PLANE
    return [planes[0]] + [
        lax.ppermute(plane, "tm", [(i, i ^ (r * PLANE)) for i in range(count)])
        for r, plane in enumerate(planes)
        if r
    ]


def within_plane(came):
    count = len(came) * PLANE
    left = regroup(came)
    return [left[0]] + [
        lax.ppermute(block, "tm", [(i, i ^ q) for i in range(count)])
        for q, block in enumerate(left)
        if q
    ]


def spectra_kernel(side, halo, own, kept, taps, table, *refs):
    out, made, go = refs[-3:]
    groups, parts = out.shape[0], out.shape[2]
    depth = TAPS - 1
    half = WIDTH // 2
    sends = []
    for k in range(half // LANES):
        cols = slice(k * LANES, (k + 1) * LANES)
        halos = [halo[t, :, cols] for t in range(depth)]
        if side:
            ends = lax.axis_index("tm") == lax.axis_size("tm") - 1
            frames = [own[t, :, cols] for t in range(1, depth)] + [kept[:, cols]]
            pool = [jnp.where(ends, jnp.zeros_like(frame), frame) for frame in frames] + halos
        else:
            pool = halos + [kept[:, cols]] + [own[t, :, cols] for t in range(depth - 1)]
        for s in range(depth):
            spectrum = jnp.dot(
                table[...],
                filtered_frame(taps, pool[s : s + TAPS], LANES),
                preferred_element_type=jnp.float32,
            ).astype(jnp.bfloat16)
            for q in range(parts):
                for g in range(groups):
                    at = (q * groups + g) * ROWS
                    made[k, g, s, q] = spectrum[at : at + ROWS]
        to = slice(side * half + k * LANES, side * half + (k + 1) * LANES)
        sends.append(pltpu.make_async_copy(made.at[k], out.at[:, :, :, :, to], go.at[k]))
        sends[-1].start()
    for copy in sends:
        copy.wait()


def later_spectra(side, halo, own, kept, taps, table, groups, parts, so_far):
    depth = TAPS - 1
    frame, cols = kept.shape
    more = [] if so_far is None else [so_far]
    return pl.pallas_call(
        functools.partial(spectra_kernel, side),
        in_specs=[INSIDE] * 5 + [ANYWHERE] * len(more),
        out_specs=ANYWHERE,
        out_shape=pltpu.HBM((groups, depth, parts, ROWS, WIDTH), jnp.bfloat16),
        scratch_shapes=[
            pltpu.VMEM((cols // LANES, groups, depth, parts, ROWS, LANES), jnp.bfloat16),
            pltpu.SemaphoreType.DMA((cols // LANES,)),
        ],
        input_output_aliases={5: 0} if more else {},
        compiler_params=pltpu.CompilerParams(vmem_limit_bytes=VMEM // 6),
        cost_estimate=pl.CostEstimate(
            flops=200 * depth * frame * frame * cols, bytes_accessed=6 << 20, transcendentals=0
        ),
        name="later_spectra",
    )(halo, own, kept, taps, table, *more)


def correlate_kernel(scale, blocks, *refs):
    sources, rest, orders = refs[:PLANE], refs[PLANE], refs[PLANE + 1]
    out, plain, turned, across, made, first, go, come = refs[-8:]
    groups, depth, parts = rest.shape[0], rest.shape[1], rest.shape[2]
    half = WIDTH // 2
    per = ROWS // 2
    pairs = 256 // ROWS
    width = 256 // per
    arrive = [
        pltpu.make_async_copy(source, first.at[q], come.at[q]) for q, source in enumerate(sources)
    ]
    for copy in arrive:
        copy.start()
    here = [(q, r) for q in range(PLANE) for r in range(groups // PLANE)]
    there = [(g, t) for g in range(groups) for t in range(depth)]
    lead = len(here) // pairs
    total = lead + len(there) // pairs

    def sending(part, f):
        return pltpu.make_async_copy(
            made.at[part, f], out.at[:, :, part * per + f], go.at[part, f]
        )

    for part in range(parts):
        for n in list(range(lead, total)) + list(range(lead)):
            if n == 0 and part == 0:
                for copy in arrive:
                    copy.wait()
            for k in range(WIDTH // LANES):
                cols = slice(k * LANES, (k + 1) * LANES)
                if n < lead:
                    rows = [
                        first[q, r, part, :, cols] for q, r in here[n * pairs : (n + 1) * pairs]
                    ]
                else:
                    some = there[(n - lead) * pairs : (n - lead + 1) * pairs]
                    behind = int(cols.start >= half)
                    rows = [rest[(g - behind) % groups, t, part, :, cols] for g, t in some]
                moved = jnp.dot(
                    orders[...], jnp.concatenate(rows, axis=0), preferred_element_type=jnp.float32
                ).astype(jnp.bfloat16)
                for f in range(per):
                    at = f * width
                    plain[f, n * width : (n + 1) * width, cols] = moved[at : at + width]
                    turned[f, n * width : (n + 1) * width, cols] = moved[
                        256 + at : 256 + at + width
                    ]

        @pl.loop(0, per, unroll=4)
        def _(f):
            across[f % 2] = plain[f].T
            for b in range(blocks.shape[1]):
                a, w = (pl.multiple_of(blocks[i, b], PANEL) for i in range(2))
                product = jnp.dot(
                    across[f % 2, pl.ds(a, PANEL), :],
                    jnp.concatenate(
                        [plain[f, :, pl.ds(w, PANEL)], turned[f, :, pl.ds(w, PANEL)]], axis=1
                    ),
                    preferred_element_type=jnp.float32,
                )
                made[part, f, b, 0] = product[:, :PANEL] * scale
                made[part, f, b, 1] = product[:, PANEL:] * scale
            sending(part, f).start()

    for part in range(parts):

        @pl.loop(0, per)
        def _(f):
            sending(part, f).wait()


def correlate(places, first, rest, orders, blocks):
    groups, depth, parts = rest.shape[0], rest.shape[1], rest.shape[2]
    per = ROWS // 2
    keys = 2 * groups * TAPS
    shape = (blocks, 2, parts * per, PANEL, PANEL)
    anywhere = pl.BlockSpec(memory_space=pl.ANY)
    inside = pl.BlockSpec(memory_space=pltpu.VMEM)
    return pl.pallas_call(
        functools.partial(correlate_kernel, 1.0 / (groups * TAPS)),
        grid_spec=pltpu.PrefetchScalarGridSpec(
            num_scalar_prefetch=1,
            grid=(1,),
            in_specs=[anywhere] * PLANE
            + [inside, inside],
            out_specs=anywhere,
            scratch_shapes=[
                pltpu.VMEM((per, keys, WIDTH), jnp.bfloat16),
                pltpu.VMEM((per, keys, WIDTH), jnp.bfloat16),
                pltpu.VMEM((2, WIDTH, keys), jnp.bfloat16),
                pltpu.VMEM((parts, per, blocks, 2, PANEL, PANEL), jnp.float32),
                pltpu.VMEM((PLANE, *first[0].shape), jnp.bfloat16),
                pltpu.SemaphoreType.DMA((parts, per)),
                pltpu.SemaphoreType.DMA((PLANE,)),
            ],
        ),
        out_shape=pltpu.HBM(shape, jnp.float32),
        compiler_params=pltpu.CompilerParams(vmem_limit_bytes=VMEM * 5//6),
        cost_estimate=pl.CostEstimate(
            flops=4 * parts * per * keys * PANEL * PANEL * blocks,
            bytes_accessed=36 << 20,
            transcendentals=0,
        ),
        name="correlate",
    )(places, *pin(*first), rest, orders)


def body(voltages, panel_map, block_list):
    groups = lax.axis_size("tm")
    own = CHANNELS // groups
    parts = own * 2 // ROWS
    frames = voltages.reshape(-1, FRAME, voltages.shape[1])
    taps = filter_taps()
    table = dft_table(groups, parts)
    block_list = block_list.T
    up, hot0, volts, places = select(0, block_list, panel_map, frames)
    earlier = shifted(up, "tm", 1, False)
    down, hot1 = select(1, block_list, panel_map, volts)
    later = shifted(down, "tm", -1, True)
    left, right, taps, table, orders, *planes = first_spectra(
        volts, (hot0, hot1), up, down, taps, table, row_orders(), groups, parts
    )
    came = across_planes(planes)
    later_half = functools.partial(
        later_spectra, taps=taps, table=table, groups=groups, parts=parts
    )
    rest = later_half(0, earlier, up, left, so_far=None)
    rest = later_half(1, later, down, right, so_far=rest)


    first = within_plane(came)
    rest = lax.all_to_all(rest, "tm", split_axis=0, concat_axis=0, tiled=True)
    return correlate(places, first, rest, orders, block_list.shape[1])


def solution(mesh):
    in_specs = (P(("band", "tm"), None), P(), P())
    out_specs = P("band", None, "tm", None, None)
    return jax.shard_map(body, mesh=mesh, in_specs=in_specs, out_specs=out_specs, check_vma=False)
```

```python
import functools

import jax
import jax.numpy as jnp
import numpy as np
from jax import lax
from jax.experimental import pallas as pl
from jax.experimental.pallas import tpu as pltpu
from jax.sharding import PartitionSpec as P

CHANNELS = 256
TAPS = 4
PANEL = 128
USED = 8
FRAME = 2 * CHANNELS
WIDTH = USED * PANEL
ROWS = 16
PLANE = 4
LANES = 256
VMEM = 60 << 20


def pin(*arrays):
    return [pltpu.with_memory_space_constraint(array, pltpu.HBM) for array in arrays]


def shifted(block, axis, distance, around):
    count = lax.axis_size(axis)
    route = [(i, (i + distance) % count) for i in range(count) if around or 0 <= i + distance < count]
    return lax.ppermute(block, axis, route)


def filter_taps():
    length = TAPS * FRAME
    place = np.arange(length, dtype=np.float64)
    middle = (length - 1) / 2.0
    window = 0.5 - 0.5 * np.cos(2.0 * np.pi * (place + 0.5) / length)
    shape_h = np.sinc((place - middle) / FRAME) * window
    shape_h = shape_h / np.sqrt(np.sum(shape_h * shape_h))
    taps = shape_h.reshape(TAPS, FRAME, 1).astype(np.float32)
    return np.broadcast_to(taps, (TAPS, FRAME, PANEL)).copy()


def dft_table(groups, parts):
    own = CHANNELS // groups
    per = own // parts
    q, g, f, c = np.meshgrid(
        np.arange(parts), np.arange(groups), np.arange(per), np.arange(2), indexing="ij"
    )
    channel = (g * own + q * per + f).reshape(-1)
    imaginary = c.reshape(-1)
    phase = (channel[:, None] * np.arange(FRAME)[None, :] % FRAME) * (2.0 * np.pi / FRAME)
    table = np.where(imaginary[:, None] == 1, -np.sin(phase), np.cos(phase))
    return table.astype(np.float32).astype(jnp.bfloat16)


def row_orders():
    pairs = 256 // ROWS
    half = ROWS // 2
    table = np.zeros((512, 256), np.float32)
    for j in range(pairs):
        for f in range(half):
            row, col = f * pairs * 2 + j * 2, j * ROWS + f * 2
            table[row, col] = 1.0
            table[row + 1, col + 1] = 1.0
            table[256 + row, col + 1] = -1.0
            table[256 + row + 1, col] = 1.0
    return table.astype(jnp.bfloat16)


def named_panels(blocks):
    bits = jnp.int32(0)
    for b in range(blocks.shape[1]):
        bits = bits | (jnp.int32(1) << blocks[0, b])
    return bits


def filtered_frame(taps_ref, frames, cols):
    total = None
    taps = [jnp.tile(taps_ref[t], (1, cols // PANEL)) for t in range(TAPS)]
    for t in range(TAPS):
        term = taps[t] * frames[t].astype(jnp.float32)
        total = term if total is None else total + term
    return total.astype(jnp.bfloat16)


def choose(side, blocks, names, hot, panels):
    bits = named_panels(blocks)
    slot = jnp.int32(0)
    slots = TAPS * USED
    for p in range(names.shape[0]):
        panels[slot] = p
        panels[slots + p] = slot * PANEL
        slot = slot + ((bits >> p) & 1)
    for j in range(USED // 2):
        wanted = names[pl.ds(panels[side * USED // 2 + j], 1), :]
        rows = lax.broadcasted_iota(jnp.int32, (hot.shape[0], PANEL), 0)
        hot[:, j * PANEL : (j + 1) * PANEL] = (
            (rows == wanted).astype(jnp.float32).astype(jnp.bfloat16)
        )


def left_kernel(listing, frames, inputs, halo, hot, volts, places, names, panels, blocks, come):
    wanted = pltpu.make_async_copy(listing, blocks, come.at[TAPS + 1])
    wanted.start()
    listed = pltpu.make_async_copy(inputs, names, come.at[TAPS])
    listed.start()
    order = list(range(1, TAPS)) + [0]
    arrive = [pltpu.make_async_copy(frames.at[t], volts.at[t], come.at[t]) for t in order]
    for copy in arrive[:-1]:
        copy.start()
    wanted.wait()
    listed.wait()
    choose(0, blocks, names, hot, panels)
    for k in range(TAPS - 1):
        arrive[k].wait()
        if k == 0:
            arrive[-1].start()
        halo[k] = jnp.dot(volts[k + 1], hot[...], preferred_element_type=jnp.float32).astype(
            jnp.bfloat16
        )
    for i in range(2):
        for b in range(blocks.shape[1]):
            places[i, b] = panels[TAPS * USED + blocks[i, b]]
    arrive[TAPS - 1].wait()


def right_kernel(listing, volts, inputs, halo, hot, names, panels, blocks, come):
    wanted = pltpu.make_async_copy(listing, blocks, come.at[TAPS + 1])
    wanted.start()
    listed = pltpu.make_async_copy(inputs, names, come.at[TAPS])
    listed.start()
    wanted.wait()
    listed.wait()
    choose(1, blocks, names, hot, panels)
    for k in range(TAPS - 1):
        halo[k] = jnp.dot(volts[k], hot[...], preferred_element_type=jnp.float32).astype(
            jnp.bfloat16
        )


ANYWHERE = pl.BlockSpec(memory_space=pl.ANY)
INSIDE = pl.BlockSpec(memory_space=pltpu.VMEM)


def select(side, block_list, panel_map, frames):
    count, frame, width = frames.shape
    depth = TAPS - 1
    half = WIDTH // 2
    out_specs = [INSIDE, INSIDE]
    out_shape = [
        pltpu.VMEM((depth, frame, half), jnp.bfloat16),
        pltpu.VMEM((width, half), jnp.bfloat16),
    ]
    if side == 0:
        out_specs += [INSIDE, pl.BlockSpec(memory_space=pltpu.SMEM)]
        out_shape += [
            pltpu.VMEM(frames.shape, jnp.bfloat16),
            jax.ShapeDtypeStruct(block_list.shape, jnp.int32),
        ]
    return pl.pallas_call(
        right_kernel if side else left_kernel,
        in_specs=[ANYWHERE, INSIDE if side else ANYWHERE, ANYWHERE],
        out_specs=out_specs,
        scratch_shapes=[
            pltpu.VMEM((width // PANEL, PANEL), jnp.int32),
            pltpu.SMEM((TAPS * USED + width // PANEL,), jnp.int32),
            pltpu.SMEM(block_list.shape, jnp.int32),
            pltpu.SemaphoreType.DMA((2 + TAPS,)),
        ],
        out_shape=out_shape,
        compiler_params=pltpu.CompilerParams(vmem_limit_bytes=VMEM // 2),
        cost_estimate=pl.CostEstimate(
            flops=depth * frame * width * WIDTH, bytes_accessed=10 << 20, transcendentals=0
        ),
        name="select",
    )(*pin(block_list), *([frames] if side else pin(frames)), *pin(panel_map.reshape(-1, PANEL)))


def first_kernel(count, volts, hot0, hot1, up, down, taps, table, orders, *refs):
    kept, held, planes = refs[:2], refs[2:5], refs[5 : 5 + count]
    spectra, come, go = refs[5 + count :]
    weights, matrix, _ = held
    groups, parts = spectra.shape[0], spectra.shape[1]
    half = WIDTH // 2
    arrive = [
        pltpu.make_async_copy(source, target, come.at[i])
        for i, (source, target) in enumerate(zip((taps, table, orders), held))
    ]
    for copy in arrive:
        copy.start()
    for side, (hot, halo) in enumerate(((hot0, up), (hot1, down))):
        kept[side][...] = jnp.dot(
            volts[side * (TAPS - 1)], hot[...], preferred_element_type=jnp.float32
        ).astype(jnp.bfloat16)
        if side == 0:
            for copy in arrive:
                copy.wait()
        for k in range(half // LANES):
            cols = slice(k * LANES, (k + 1) * LANES)
            pool = [halo[t, :, cols] for t in range(TAPS - 1)]
            pool.insert(side * (TAPS - 1), kept[side][:, cols])
            spectrum = jnp.dot(
                matrix[...],
                filtered_frame(weights, pool, LANES),
                preferred_element_type=jnp.float32,
            ).astype(jnp.bfloat16)
            at_cols = slice(side * half + k * LANES, side * half + (k + 1) * LANES)
            for q in range(parts):
                for g in range(groups):
                    at = (q * groups + g) * ROWS
                    spectra[g, q, :, at_cols] = spectrum[at : at + ROWS]
    mine = lax.axis_index("tm") // PLANE
    sends = [
        pltpu.make_async_copy(spectra.at[pl.ds((mine ^ r) * PLANE, PLANE)], plane, go.at[r])
        for r, plane in enumerate(planes)
    ]
    for copy in sends:
        copy.start()
    for copy in sends:
        copy.wait()


def first_spectra(volts, hots, up, down, taps, table, orders, groups, parts):
    count, frame, width = volts.shape
    half = WIDTH // 2
    planes = groups // PLANE
    return pl.pallas_call(
        functools.partial(first_kernel, planes),
        in_specs=[INSIDE] * 5 + [ANYWHERE] * 3,
        out_specs=[INSIDE] * 5 + [ANYWHERE] * planes,
        scratch_shapes=[
            pltpu.VMEM((groups, parts, ROWS, WIDTH), jnp.bfloat16),
            pltpu.SemaphoreType.DMA((3,)),
            pltpu.SemaphoreType.DMA((planes,)),
        ],
        out_shape=[pltpu.VMEM((frame, half), jnp.bfloat16)] * 2
        + [pltpu.VMEM(held.shape, held.dtype) for held in (taps, table, orders)]
        + [pltpu.HBM((PLANE, parts, ROWS, WIDTH), jnp.bfloat16)] * planes,
        compiler_params=pltpu.CompilerParams(vmem_limit_bytes=VMEM // 2),
        cost_estimate=pl.CostEstimate(
            flops=2 * frame * (width + frame) * WIDTH, bytes_accessed=16 << 20, transcendentals=0
        ),
        name="first_spectra",
    )(volts, *hots, up, down, *pin(taps, table, orders))


def regroup_kernel(*refs):
    planes = len(refs) - 3 - PLANE
    came, left, (held, come, go) = refs[:planes], refs[planes:-3], refs[-3:]
    mine = lax.axis_index("tm") % PLANE
    arrive = [
        [
            pltpu.make_async_copy(plane.at[mine ^ q], held.at[q, r], come.at[q, r])
            for r, plane in enumerate(came)
        ]
        for q in range(PLANE)
    ]
    leave = [pltpu.make_async_copy(held.at[q], left[q], go.at[q]) for q in range(PLANE)]
    for copies in arrive:
        for copy in copies:
            copy.start()
    for copies, copy in zip(arrive, leave):
        for part in copies:
            part.wait()
        copy.start()
    for copy in leave:
        copy.wait()


def regroup(came):
    planes = len(came)
    shape = (planes, *came[0].shape[1:])
    anywhere = pl.BlockSpec(memory_space=pl.ANY)
    return pl.pallas_call(
        regroup_kernel,
        in_specs=[anywhere] * planes,
        out_specs=[anywhere] * PLANE,
        scratch_shapes=[
            pltpu.VMEM((PLANE, *shape), jnp.bfloat16),
            pltpu.SemaphoreType.DMA((PLANE, planes)),
            pltpu.SemaphoreType.DMA((PLANE,)),
        ],
        out_shape=[pltpu.HBM(shape, jnp.bfloat16)] * PLANE,
        compiler_params=pltpu.CompilerParams(vmem_limit_bytes=VMEM // 12),
        cost_estimate=pl.CostEstimate(flops=1 << 37, bytes_accessed=2 << 20, transcendentals=0),
        name="regroup",
    )(*came)


def across_planes(planes):
    count = len(planes) * PLANE
    return [planes[0]] + [
        lax.ppermute(plane, "tm", [(i, i ^ (r * PLANE)) for i in range(count)])
        for r, plane in enumerate(planes)
        if r
    ]


def within_plane(came):
    count = len(came) * PLANE
    left = regroup(came)
    return [left[0]] + [
        lax.ppermute(block, "tm", [(i, i ^ q) for i in range(count)])
        for q, block in enumerate(left)
        if q
    ]


def spectra_kernel(side, halo, own, kept, taps, table, *refs):
    out, made, go = refs[-3:]
    groups, parts = out.shape[0], out.shape[2]
    depth = TAPS - 1
    half = WIDTH // 2
    sends = []
    for k in range(half // LANES):
        cols = slice(k * LANES, (k + 1) * LANES)
        halos = [halo[t, :, cols] for t in range(depth)]
        if side:
            ends = lax.axis_index("tm") == lax.axis_size("tm") - 1
            frames = [own[t, :, cols] for t in range(1, depth)] + [kept[:, cols]]
            pool = [jnp.where(ends, jnp.zeros_like(frame), frame) for frame in frames] + halos
        else:
            pool = halos + [kept[:, cols]] + [own[t, :, cols] for t in range(depth - 1)]
        for s in range(depth):
            spectrum = jnp.dot(
                table[...],
                filtered_frame(taps, pool[s : s + TAPS], LANES),
                preferred_element_type=jnp.float32,
            ).astype(jnp.bfloat16)
            for q in range(parts):
                for g in range(groups):
                    at = (q * groups + g) * ROWS
                    made[k, g, s, q] = spectrum[at : at + ROWS]
        to = slice(side * half + k * LANES, side * half + (k + 1) * LANES)
        sends.append(pltpu.make_async_copy(made.at[k], out.at[:, :, :, :, to], go.at[k]))
        sends[-1].start()
    for copy in sends:
        copy.wait()


def later_spectra(side, halo, own, kept, taps, table, groups, parts, so_far):
    depth = TAPS - 1
    frame, cols = kept.shape
    more = [] if so_far is None else [so_far]
    return pl.pallas_call(
        functools.partial(spectra_kernel, side),
        in_specs=[INSIDE] * 5 + [ANYWHERE] * len(more),
        out_specs=ANYWHERE,
        out_shape=pltpu.HBM((groups, depth, parts, ROWS, WIDTH), jnp.bfloat16),
        scratch_shapes=[
            pltpu.VMEM((cols // LANES, groups, depth, parts, ROWS, LANES), jnp.bfloat16),
            pltpu.SemaphoreType.DMA((cols // LANES,)),
        ],
        input_output_aliases={5: 0} if more else {},
        compiler_params=pltpu.CompilerParams(vmem_limit_bytes=VMEM // 6),
        cost_estimate=pl.CostEstimate(
            flops=200 * depth * frame * frame * cols, bytes_accessed=6 << 20, transcendentals=0
        ),
        name="later_spectra",
    )(halo, own, kept, taps, table, *more)


def correlate_kernel(scale, blocks, *refs):
    sources, rest, orders = refs[:PLANE], refs[PLANE], refs[PLANE + 1]
    out, plain, turned, across, made, first, go, come = refs[-8:]
    groups, depth, parts = rest.shape[0], rest.shape[1], rest.shape[2]
    half = WIDTH // 2
    per = ROWS // 2
    pairs = 256 // ROWS
    width = 256 // per
    arrive = [
        pltpu.make_async_copy(source, first.at[q], come.at[q]) for q, source in enumerate(sources)
    ]
    for copy in arrive:
        copy.start()
    here = [(q, r) for q in range(PLANE) for r in range(groups // PLANE)]
    there = [(g, t) for g in range(groups) for t in range(depth)]
    lead = len(here) // pairs
    total = lead + len(there) // pairs

    def sending(part, f):
        return pltpu.make_async_copy(
            made.at[part, f], out.at[:, :, part * per + f], go.at[part, f]
        )

    for part in range(parts):
        for n in list(range(lead, total)) + list(range(lead)):
            if n == 0 and part == 0:
                for copy in arrive:
                    copy.wait()
            for k in range(WIDTH // LANES):
                cols = slice(k * LANES, (k + 1) * LANES)
                if n < lead:
                    rows = [
                        first[q, r, part, :, cols] for q, r in here[n * pairs : (n + 1) * pairs]
                    ]
                else:
                    some = there[(n - lead) * pairs : (n - lead + 1) * pairs]
                    behind = int(cols.start >= half)
                    rows = [rest[(g - behind) % groups, t, part, :, cols] for g, t in some]
                moved = jnp.dot(
                    orders[...], jnp.concatenate(rows, axis=0), preferred_element_type=jnp.float32
                ).astype(jnp.bfloat16)
                for f in range(per):
                    at = f * width
                    plain[f, n * width : (n + 1) * width, cols] = moved[at : at + width]
                    turned[f, n * width : (n + 1) * width, cols] = moved[
                        256 + at : 256 + at + width
                    ]

        @pl.loop(0, per, unroll=8)
        def _(f):
            across[f % 2] = plain[f].T
            for b in range(blocks.shape[1]):
                a, w = (pl.multiple_of(blocks[i, b], PANEL) for i in range(2))
                product = jnp.dot(
                    across[f % 2, pl.ds(a, PANEL), :],
                    jnp.concatenate(
                        [plain[f, :, pl.ds(w, PANEL)], turned[f, :, pl.ds(w, PANEL)]], axis=1
                    ),
                    preferred_element_type=jnp.float32,
                )
                made[part, f, b, 0] = product[:, :PANEL] * scale
                made[part, f, b, 1] = product[:, PANEL:] * scale
            sending(part, f).start()

    for part in range(parts):

        @pl.loop(0, per)
        def _(f):
            sending(part, f).wait()


def correlate(places, first, rest, orders, blocks):
    groups, depth, parts = rest.shape[0], rest.shape[1], rest.shape[2]
    per = ROWS // 2
    keys = 2 * groups * TAPS
    shape = (blocks, 2, parts * per, PANEL, PANEL)
    anywhere = pl.BlockSpec(memory_space=pl.ANY)
    inside = pl.BlockSpec(memory_space=pltpu.VMEM)
    return pl.pallas_call(
        functools.partial(correlate_kernel, 1.0 / (groups * TAPS)),
        grid_spec=pltpu.PrefetchScalarGridSpec(
            num_scalar_prefetch=1,
            grid=(1,),
            in_specs=[anywhere] * PLANE
            + [inside, inside],
            out_specs=anywhere,
            scratch_shapes=[
                pltpu.VMEM((per, keys, WIDTH), jnp.bfloat16),
                pltpu.VMEM((per, keys, WIDTH), jnp.bfloat16),
                pltpu.VMEM((2, WIDTH, keys), jnp.bfloat16),
                pltpu.VMEM((parts, per, blocks, 2, PANEL, PANEL), jnp.float32),
                pltpu.VMEM((PLANE, *first[0].shape), jnp.bfloat16),
                pltpu.SemaphoreType.DMA((parts, per)),
                pltpu.SemaphoreType.DMA((PLANE,)),
            ],
        ),
        out_shape=pltpu.HBM(shape, jnp.float32),
        compiler_params=pltpu.CompilerParams(vmem_limit_bytes=VMEM * 5//6),
        cost_estimate=pl.CostEstimate(
            flops=4 * parts * per * keys * PANEL * PANEL * blocks,
            bytes_accessed=36 << 20,
            transcendentals=0,
        ),
        name="correlate",
    )(places, *pin(*first), rest, orders)


def body(voltages, panel_map, block_list):
    groups = lax.axis_size("tm")
    own = CHANNELS // groups
    parts = own * 2 // ROWS
    frames = voltages.reshape(-1, FRAME, voltages.shape[1])
    taps = filter_taps()
    table = dft_table(groups, parts)
    block_list = block_list.T
    up, hot0, volts, places = select(0, block_list, panel_map, frames)
    earlier = shifted(up, "tm", 1, False)
    down, hot1 = select(1, block_list, panel_map, volts)
    later = shifted(down, "tm", -1, True)
    left, right, taps, table, orders, *planes = first_spectra(
        volts, (hot0, hot1), up, down, taps, table, row_orders(), groups, parts
    )
    came = across_planes(planes)
    later_half = functools.partial(
        later_spectra, taps=taps, table=table, groups=groups, parts=parts
    )
    rest = later_half(0, earlier, up, left, so_far=None)
    rest = later_half(1, later, down, right, so_far=rest)


    first = within_plane(came)
    rest = lax.all_to_all(rest, "tm", split_axis=0, concat_axis=0, tiled=True)
    return correlate(places, first, rest, orders, block_list.shape[1])


def solution(mesh):
    in_specs = (P(("band", "tm"), None), P(), P())
    out_specs = P("band", None, "tm", None, None)
    return jax.shard_map(body, mesh=mesh, in_specs=in_specs, out_specs=out_specs, check_vma=False)
```
